256 devices in a mesh: tm: 4 (over y), tile: 64 (over z, x, core).
Axes of the slice: x: 4, y: 4, z: 8, core: 2. Of those that a mesh axis runs over, the one named last changes fastest.
Arguments:
- states: float32 [4, 16, 256, 256], P('tm', None, 'tile'), may hold values from -6 to 6
- increments: float32 [4, 16, 256, 256], P('tm', None, 'tile'), may hold values from -6 to 6
- w_first: bfloat16 [9, 16, 128], replicated, may hold values from -0.5 to 0.5
- w_mid: bfloat16 [2, 9, 128, 128], replicated, may hold values from -0.1875 to 0.1875
- w_last: bfloat16 [9, 16, 128], replicated, may hold values from -0.1875 to 0.1875
- biases: float32 [3, 128], replicated, may hold values from -2 to 2
- cov_x: float32 [256, 256], replicated, may hold values from -4 to 24, as said below
- cov_y: float32 [256, 256], replicated, may hold values from -4 to 24, as said below
Outputs:
- multiplier: float32 [4, 16, 256, 256], P('tm', None, 'tile')
- update: float32 [4, 16, 256, 256], P('tm', None, 'tile')
The draws below stay inside these ranges and needn't reach their ends.
Inputs may be any that keep to these rules, and one draw needn't show every extreme that they name: `cov_x`: symmetric positive definite. `cov_y`: symmetric positive definite.
All inputs are finite; a program needn't handle non-finite values.
Results may differ from the reference program's by a relative error of at most 0.0024.
Values may be sent and summed in bfloat16 or wider, within the bound.
A program may use at most 64 MiB of HBM per device.

```python
import jax
import jax.numpy as jnp
from jax import lax

F = 16
C = 128
NX = 256
NY = 256
SUBWINDOWS = 4


def covariance(key, order):
    key_length = jax.random.fold_in(key, 1)
    key_mixing = jax.random.fold_in(key, 2)
    length = jax.random.uniform(key_length, (), jnp.float32, 24.0, 64.0)
    positions = jnp.arange(order).astype(jnp.float32)
    kernel = jnp.exp(-jnp.abs(positions[:, None] - positions[None, :]) / length) / jnp.sqrt(length)
    mixing = jax.random.normal(key_mixing, (order, order), jnp.float32) / jnp.sqrt(order * 1.0)
    result = 0.5 * kernel + 0.5 * jnp.dot(mixing, mixing.T, precision=lax.Precision.HIGHEST)
    return result


def draw_cov_x(key, part):
    return covariance(jax.random.fold_in(key, 11), NX)


def draw_cov_y(key, part):
    return covariance(jax.random.fold_in(key, 12), NY)


def block_scale(stream_key, extent, cuts, low, high):
    factor_of = 1.0
    for axis_at, shards_of in cuts:
        heights = jax.random.uniform(jax.random.fold_in(jax.random.fold_in(stream_key, 6), axis_at), (shards_of,), jnp.float32, low / len(cuts), high / len(cuts))
        factor_of = factor_of * jnp.repeat(jnp.exp(heights), extent[axis_at] // shards_of).reshape((-1,) + (1,) * (len(extent) - 1 - axis_at))
    return factor_of


def centred(key, extent, deviation, most, cuts=(), held_as=jnp.bfloat16):
    values = deviation * jax.random.normal(key, extent, jnp.float32)
    if cuts:
        values = values * block_scale(key, extent, cuts, -0.22, 0.18)
    return jnp.clip(values, -most, most).astype(held_as)


def setup_inputs(seed: int = 0) -> dict:
    seeds = jax.random.split(jax.random.key(seed), 9)
    states = centred(seeds[0], (SUBWINDOWS, F, NX, NY), 1.0, 6.0, ((0, 4), (2, 64)), jnp.float32)
    increments = centred(seeds[1], (SUBWINDOWS, F, NX, NY), 1.0, 6.0, ((0, 4), (2, 64)), jnp.float32)
    w_first = centred(seeds[2], (9, F, C), (9 * F) ** -0.5, 0.5)
    w_mid = centred(seeds[3], (2, 9, C, C), (9 * C) ** -0.5, 0.1875)
    w_last = centred(seeds[4], (9, F, C), (9 * C) ** -0.5, 0.1875)
    biases = centred(seeds[5], (3, C), 0.5, 2.0, (), jnp.float32)
    cov_x = draw_cov_x(jax.random.fold_in(seeds[8], 71), 0)
    cov_y = draw_cov_y(jax.random.fold_in(seeds[8], 71), 0)
    return {"states": states, "increments": increments, "w_first": w_first, "w_mid": w_mid, "w_last": w_last, "biases": biases, "cov_x": cov_x, "cov_y": cov_y}


def convolve(padded, kernel, pattern, flipped):
    height = padded.shape[2] - 2
    across = padded.shape[3]
    widened = jnp.pad(padded, ((0, 0), (0, 0), (0, 0), (1, 1)))
    summed = None
    for tap_index in range(9):
        row_off = tap_index // 3
        col_off = tap_index % 3
        if flipped:
            row_off = 2 - row_off
            col_off = 2 - col_off
        window = widened[:, :, row_off:row_off + height, col_off:col_off + across]
        contribution = jnp.einsum(pattern, kernel[tap_index].astype(jnp.float32), window.astype(jnp.float32))
        summed = contribution if summed is None else summed + contribution
    return summed


def pad_rows(values):
    return jnp.pad(values, ((0, 0), (0, 0), (1, 1), (0, 0)))


def forward_slopes(state_one, w_first, w_mid, biases):
    kernels = (w_first, w_mid[0], w_mid[1])
    current = state_one.astype(jnp.bfloat16)
    slopes = []
    for layer_index in range(3):
        combined = convolve(pad_rows(current), kernels[layer_index], "co,scxy->soxy", False)
        primal = jnp.tanh(combined + biases[layer_index][None, :, None, None])
        slopes.append(1.0 - primal * primal)
        current = primal.astype(jnp.bfloat16)
    return slopes


def tangent_pass(state_one, incr_one, w_first, w_mid, w_last, biases):
    kernels = (w_first, w_mid[0], w_mid[1])
    slopes = forward_slopes(state_one, w_first, w_mid, biases)
    tangent = incr_one.astype(jnp.bfloat16)
    for layer_index in range(3):
        combined = convolve(pad_rows(tangent), kernels[layer_index], "co,scxy->soxy", False)
        tangent = (slopes[layer_index] * combined).astype(jnp.bfloat16)
    return convolve(pad_rows(tangent), w_last, "oc,scxy->soxy", False)


def adjoint_pass(state_one, mult_one, w_first, w_mid, w_last, biases):
    kernels = (w_first, w_mid[0], w_mid[1])
    slopes = forward_slopes(state_one, w_first, w_mid, biases)
    cotangent = mult_one.astype(jnp.bfloat16)
    backward = convolve(pad_rows(cotangent), w_last, "oc,soxy->scxy", True)
    for layer_index in (2, 1, 0):
        cotangent = (slopes[layer_index] * backward).astype(jnp.bfloat16)
        backward = convolve(pad_rows(cotangent), kernels[layer_index], "co,soxy->scxy", True)
    return backward


def reference(states, increments, w_first, w_mid, w_last, biases, cov_x, cov_y):
    change = lax.map(lambda paired: tangent_pass(paired[0][None], paired[1][None], w_first, w_mid, w_last, biases)[0], (states, increments))
    shifted_up = jnp.concatenate((increments[1:], jnp.zeros_like(increments[:1])), axis=0)
    misfit = shifted_up - increments - change
    smoothed = jnp.einsum("kfxy,zy->kfxz", misfit, cov_y, precision=lax.Precision.HIGHEST)
    multiplier = jnp.einsum("ij,kfjz->kfiz", cov_x, smoothed, precision=lax.Precision.HIGHEST)
    backward = lax.map(lambda paired: adjoint_pass(paired[0][None], paired[1][None], w_first, w_mid, w_last, biases)[0], (states, multiplier))
    behind = jnp.concatenate((jnp.zeros_like(multiplier[:1]), multiplier[:-1]), axis=0)
    update = behind - multiplier - backward
    return multiplier, update
```

```python
import jax
import jax.numpy as jnp
from jax import lax
from jax.experimental import pallas as pl
from jax.experimental.pallas import tpu as pltpu
from jax.sharding import PartitionSpec as P

F32 = jnp.float32
BF16 = jnp.bfloat16
MESH = pl.DeviceIdType.MESH
TILES = 64
WINDOWS = 4
CHIPS = 32


def contract(a, b, dims=((1,), (0,))):
    return lax.dot_general(a, b, (dims, ((), ())), preferred_element_type=F32)


def split(x):
    high = x.astype(BF16)
    return high, (x - high.astype(F32)).astype(BF16)


def shifted_rows(v):
    at = lax.broadcasted_iota(jnp.int32, (8, v.shape[1]), 0)
    up = pltpu.roll(v, 1, 0)
    down = pltpu.roll(v, v.shape[0] - 1, 0)
    up = jnp.concatenate([jnp.where(at == 0, 0.0, up[:8]), up[8:]], axis=0)
    down = jnp.concatenate([down[:-8], jnp.where(at == 7, 0.0, down[-8:])], axis=0)
    return up, down


def shifted_lanes(v):
    at = lax.broadcasted_iota(jnp.int32, v.shape, 1)
    n = v.shape[1]
    up = jnp.where(at == 0, 0.0, pltpu.roll(v, 1, 1))
    down = jnp.where(at == n - 1, 0.0, pltpu.roll(v, n - 1, 1))
    return up, down


def put_three(buf, i, v):
    up, down = shifted_rows(v)
    buf[i, :, 0:256] = up.astype(BF16)
    buf[i, :, 256:512] = v.astype(BF16)
    buf[i, :, 512:768] = down.astype(BF16)


def put_taps(buf, i, v):
    up, down = shifted_lanes(v)
    buf[i, 0:16] = up.astype(BF16)
    buf[i, 16:32] = v.astype(BF16)
    buf[i, 32:48] = down.astype(BF16)


def build_thin(dst, tap):
    zero = jnp.zeros((16, 128), BF16)
    for r in range(4):
        for q in range(3):
            for o in range(2):
                p = r - o
                at = (r * 3 + q) * 16
                block = tap(3 * p + q) if 0 <= p <= 2 else zero
                dst[at : at + 16, o * 128 : o * 128 + 128] = block


def build_wide(dst, tap):
    zero = jnp.zeros((128, 128), BF16)
    for pair in range(2):
        for q in range(3):
            for rr in range(2):
                for o in range(2):
                    p = 2 * pair + rr - o
                    at = pair * 768 + q * 256 + rr * 128
                    block = tap(3 * p + q) if 0 <= p <= 2 else zero
                    dst[at : at + 128, o * 128 : o * 128 + 128] = block


def wide_conv(buf, i, weights):
    both = jnp.concatenate([buf[i], buf[i + 1]], axis=1)
    return contract(both, weights[...])


def thin_conv(buf, i, weights):
    return contract(buf[i : i + 4].reshape(192, 256), weights[...], ((0,), (0,)))


def fold_rows(parts, r, flipped):
    sums = []
    for q in range(3):
        total = None
        for p in range(3):
            t = 3 * p + q
            t = 8 - t if flipped else t
            piece = parts[r + p][t * 16 : t * 16 + 16]
            total = piece if total is None else total + piece
        sums.append(total)
    up, _ = shifted_lanes(sums[0])
    _, down = shifted_lanes(sums[2])
    return up + sums[1] + down


def kernel(
    st, inc, wf_h, wm_h, wl_h, bias, cx_h, cy_h,
    mult_o, upd_o,
    wf, wm, wl, cx, cy,
    x, xq, tq, a1, t1, a2, t2, t3, b3, b2, b1, s1, s2, s3,
    w1, wk2, wk3, v4, vk3, vk2, cx3, cy3,
    nxt, prev, chg, sbuf, rbuf, obuf, mbuf,
    wsem, hs, hr, ns, nr, ps, pr, as_, ar, at_s, at_r, al, bs, br, bt_s, bt_r, bl,
):
    tm = lax.axis_index("tm")
    me = lax.axis_index("tile")
    chip = lax.div(me, 2)
    core = lax.rem(me, 2)
    tm_next = lax.rem(tm + 1, WINDOWS)
    tm_back = lax.rem(tm + WINDOWS - 1, WINDOWS)

    barrier = pltpu.get_barrier_semaphore()

    def greet(i, carry):
        to = lax.rem(me + i, TILES)
        pl.semaphore_signal(barrier, inc=1, device_id={"tile": to}, device_id_type=MESH)
        return carry

    lax.fori_loop(1, TILES, greet, 0)
    for to in (tm_next, tm_back):
        pl.semaphore_signal(barrier, inc=1, device_id={"tm": to}, device_id_type=MESH)

    loads = [
        pltpu.make_async_copy(src, dst, wsem.at[n])
        for n, (src, dst) in enumerate(
            ((wf_h, wf), (wm_h, wm), (wl_h, wl), (cx_h, cx), (cy_h, cy))
        )
    ]
    for load in loads:
        load.start()

    for r in range(4):
        x[6 + r, 0] = st[0, :, r, :].astype(BF16)
        x[6 + r, 1] = inc[0, :, r, :].astype(BF16)

    pl.semaphore_wait(barrier, TILES - 1 + 2)

    halo = []
    for n, (step, src, dst) in enumerate(
        (
            (1, x.at[6:10], x.at[2:6]),
            (TILES - 1, x.at[6:10], x.at[10:14]),
            (2, x.at[8:10, 0], x.at[0:2, 0]),
            (TILES - 2, x.at[6:8, 0], x.at[14:16, 0]),
        )
    ):
        halo.append(
            pltpu.make_async_remote_copy(
                src, dst, hs.at[n], hr.at[n],
                device_id={"tile": lax.rem(me + step, TILES)}, device_id_type=MESH,
            )
        )
    for copy in halo:
        copy.start()
    ahead = pltpu.make_async_remote_copy(
        inc.at[0], nxt, ns, nr, device_id={"tm": tm_back}, device_id_type=MESH
    )
    ahead.start()

    def valid(e):
        g = 4 * me - 6 + e
        return jnp.where((g >= 0) & (g < 4 * TILES), 1.0, 0.0).astype(F32)

    def pair_mask(e):
        lane = lax.broadcasted_iota(jnp.int32, (1, 256), 1)
        return jnp.where(lane < 128, valid(e), valid(e + 1))

    def inner(e):
        return e >= 6 and e + 1 <= 9

    for e in range(6, 10):
        put_taps(xq, e, x[e, 0].astype(F32))
        put_taps(tq, e, x[e, 1].astype(F32))
    loads[0].wait()
    build_thin(w1, lambda t: wf[t])
    loads[1].wait()
    build_wide(wk2, lambda t: wm[0, t])
    build_wide(wk3, lambda t: wm[1, t])
    loads[2].wait()
    build_thin(v4, lambda t: wl[8 - t])
    loads[3].wait()
    high, low = split(cx[...])
    cx3[:, 0:256] = high
    cx3[:, 256:512] = high
    cx3[:, 512:768] = low
    loads[4].wait()
    high, low = split(cy[...])
    cy3[0:256] = high
    cy3[256:512] = high
    cy3[512:768] = low
    biases = [jnp.concatenate([bias[l : l + 1], bias[l : l + 1]], axis=1) for l in range(3)]

    for copy in halo[:2]:
        copy.wait_recv()

    def edge_row(e, with_tangent):
        put_taps(xq, e, x[e, 0].astype(F32) * valid(e))
        if with_tangent:
            put_taps(tq, e, x[e, 1].astype(F32) * valid(e))

    for e in (2, 3, 4, 5, 10, 11, 12, 13):
        edge_row(e, True)

    def activation(l, z, e, s_buf, i, out):
        h = jnp.tanh(z + biases[l])
        s = 1.0 - h * h
        if not inner(e):
            mask = pair_mask(e)
            s = s * mask
            h = h * mask
        s_buf[i] = s
        if out is not None:
            put_three(out, i, h)
        return s

    def layer_one(i, tangent):
        s = activation(0, thin_conv(xq, 2 * i, w1), 2 * i + 1, s1, i, a1)
        if tangent:
            put_three(t1, i, s * thin_conv(tq, 2 * i, w1))

    def layer_two(i, tangent):
        s = activation(1, wide_conv(a1, i, wk2), 2 * i + 2, s2, i, a2)
        if tangent:
            put_three(t2, i, s * wide_conv(t1, i, wk2))

    def layer_three(i, tangent):
        s = activation(2, wide_conv(a2, i, wk3), 2 * i + 3, s3, i, None)
        if tangent:
            t3[i] = (s * wide_conv(t2, i, wk3)).astype(BF16)

    for i in range(1, 6):
        layer_one(i, True)
    for i in range(1, 5):
        layer_two(i, True)
    for i in range(1, 4):
        layer_three(i, True)

    last = wl[...].reshape(144, 128)
    parts = []
    for i in range(1, 4):
        for half in range(2):
            parts.append(contract(last, t3[i, :, half * 128 : half * 128 + 128], ((1,), (1,))))
    for r in range(4):
        chg[:, r, :] = fold_rows(parts, r, False)

    ahead.wait_recv()
    not_last = jnp.where(tm == WINDOWS - 1, 0.0, 1.0).astype(F32)
    misfit = nxt[...] * not_last - inc[0] - chg[...]
    high, low = split(misfit.reshape(64, 256))
    smoothed = contract(jnp.concatenate([high, low, high], axis=1), cy3[...])
    for half in range(2):
        sbuf[half * 16 : half * 16 + 16] = smoothed[:, half * 128 : half * 128 + 128].reshape(
            16, 4, 128
        )

    def out_chunk(i, send, recv):
        c = lax.rem(chip + i, CHIPS)
        return pltpu.make_async_remote_copy(
            sbuf.at[c], rbuf.at[me], send, recv,
            device_id={"tile": 2 * c}, device_id_type=MESH,
        )

    def start_chunk(i, carry):
        out_chunk(i, as_, ar).start()
        return carry

    lax.fori_loop(1, CHIPS, start_chunk, 0)
    own_chunk = pltpu.make_async_copy(sbuf.at[chip], rbuf.at[me], al)

    @pl.when(core == 0)
    def _():
        own_chunk.start()

    @pl.when(core == 1)
    def _():
        out_chunk(0, at_s, at_r).start()

    for copy in halo[2:]:
        copy.wait_recv()
    for e in (0, 1, 14, 15):
        edge_row(e, False)
    for i in (0, 6):
        layer_one(i, False)
    for i in (0, 5):
        layer_two(i, False)
    for i in (0, 4):
        layer_three(i, False)
    build_wide(vk3, lambda t: wm[1, 8 - t].T)
    build_wide(vk2, lambda t: wm[0, 8 - t].T)

    @pl.when(core == 0)
    def _():
        obuf[0] = jnp.zeros((4, 128), F32)
        obuf[TILES + 1] = jnp.zeros((4, 128), F32)
        own_chunk.wait()
        partner = pltpu.make_async_remote_copy(
            sbuf.at[0], rbuf.at[me + 1], at_s, at_r,
            device_id={"tile": me}, device_id_type=MESH,
        )
        partner.wait_recv()
        pltpu.make_async_copy(
            rbuf.at[0 : TILES - 2], rbuf.at[0 : TILES - 2], ar
        ).wait()
        high, low = split(rbuf[...].reshape(256, 128))
        result = contract(cx3[...], jnp.concatenate([high, low, high], axis=0))
        obuf[1 : TILES + 1] = result.reshape(TILES, 4, 128)

        def back_chunk(d, send, recv):
            return pltpu.make_async_remote_copy(
                obuf.at[pl.ds(d, 3)], mbuf.at[chip], send, recv,
                device_id={"tile": d}, device_id_type=MESH,
            )

        def start_back(i, carry):
            back_chunk(lax.rem(me + i, TILES), bs, br).start()
            return carry

        lax.fori_loop(2, TILES, start_back, 0)
        back_chunk(me + 1, bt_s, bt_r).start()
        own_back = pltpu.make_async_copy(obuf.at[pl.ds(me, 3)], mbuf.at[chip], bl)
        own_back.start()
        own_back.wait()

    @pl.when(core == 1)
    def _():
        pltpu.make_async_remote_copy(
            obuf.at[0:3], mbuf.at[chip], bt_s, bt_r,
            device_id={"tile": me}, device_id_type=MESH,
        ).wait_recv()

    pltpu.make_async_copy(mbuf.at[0 : CHIPS - 1], mbuf.at[0 : CHIPS - 1], br).wait()

    behind = pltpu.make_async_remote_copy(
        mbuf.at[:, 1], prev, ps, pr, device_id={"tm": tm_next}, device_id_type=MESH
    )
    behind.start()

    for idx in range(12):
        j, k = idx // 4, idx % 4
        row = jnp.concatenate([mbuf[0:16, j, k, :], mbuf[16:32, j, k, :]], axis=1)
        if j != 1:
            row = row * valid(2 + idx)
        put_taps(xq, idx, row.astype(BF16).astype(F32))
    for i in range(5):
        b = s3[i] * thin_conv(xq, 2 * i, v4)
        put_three(b3, i, b)
    for i in range(4):
        put_three(b2, i, s2[i + 1] * wide_conv(b3, i, vk3))
    for i in range(3):
        b1[i] = (s1[i + 2] * wide_conv(b2, i, vk2)).astype(BF16)
    first = wf[...].reshape(144, 128)
    parts = []
    for i in range(3):
        for half in range(2):
            parts.append(contract(first, b1[i, :, half * 128 : half * 128 + 128], ((1,), (1,))))
    for r in range(4):
        chg[:, r, :] = fold_rows(parts, r, True)

    behind.wait_recv()
    not_first = jnp.where(tm == 0, 0.0, 1.0).astype(F32)
    for half in range(2):
        lanes = slice(half * 128, half * 128 + 128)
        chunk = slice(half * 16, half * 16 + 16)
        own = mbuf[chunk, 1]
        mult_o[0, :, :, lanes] = own
        upd_o[0, :, :, lanes] = prev[chunk] * not_first - own - chg[:, :, lanes]

    for copy in halo:
        copy.wait_send()
    ahead.wait_send()
    behind.wait_send()
    pltpu.make_async_copy(sbuf.at[0 : CHIPS - 1], sbuf.at[0 : CHIPS - 1], as_).wait()

    @pl.when(core == 1)
    def _():
        pltpu.make_async_copy(sbuf.at[0], sbuf.at[0], at_s).wait()

    @pl.when(core == 0)
    def _():
        pltpu.make_async_copy(obuf.at[0:3], obuf.at[0:3], bt_s).wait()
        sent = mbuf.at[0 : CHIPS - 1]
        pltpu.make_async_copy(sent, sent, bs).wait()
        pltpu.make_async_copy(sent, sent, bs).wait()


def local(states, increments, w_first, w_mid, w_last, biases, cov_x, cov_y):
    vmem = pl.BlockSpec(memory_space=pltpu.VMEM)
    anywhere = pl.BlockSpec(memory_space=pl.ANY)
    dma = pltpu.SemaphoreType.DMA
    scratch = [
        pltpu.VMEM((9, 16, 128), BF16),
        pltpu.VMEM((2, 9, 128, 128), BF16),
        pltpu.VMEM((9, 16, 128), BF16),
        pltpu.VMEM((256, 256), F32),
        pltpu.VMEM((256, 256), F32),
        pltpu.VMEM((16, 2, 16, 256), BF16),
        pltpu.VMEM((16, 48, 256), BF16),
        pltpu.VMEM((16, 48, 256), BF16),
        pltpu.VMEM((7, 256, 768), BF16),
        pltpu.VMEM((7, 256, 768), BF16),
        pltpu.VMEM((6, 256, 768), BF16),
        pltpu.VMEM((6, 256, 768), BF16),
        pltpu.VMEM((5, 256, 256), BF16),
        pltpu.VMEM((5, 256, 768), BF16),
        pltpu.VMEM((4, 256, 768), BF16),
        pltpu.VMEM((3, 256, 256), BF16),
        pltpu.VMEM((7, 256, 256), F32),
        pltpu.VMEM((6, 256, 256), F32),
        pltpu.VMEM((5, 256, 256), F32),
        pltpu.VMEM((192, 256), BF16),
        pltpu.VMEM((1536, 256), BF16),
        pltpu.VMEM((1536, 256), BF16),
        pltpu.VMEM((192, 256), BF16),
        pltpu.VMEM((1536, 256), BF16),
        pltpu.VMEM((1536, 256), BF16),
        pltpu.VMEM((256, 768), BF16),
        pltpu.VMEM((768, 256), BF16),
        pltpu.VMEM((16, 4, 256), F32),
        pltpu.VMEM((32, 4, 128), F32),
        pltpu.VMEM((16, 4, 256), F32),
        pltpu.VMEM((32, 4, 128), F32),
        pltpu.VMEM((TILES, 4, 128), F32),
        pltpu.VMEM((TILES + 2, 4, 128), F32),
        pltpu.VMEM((32, 3, 4, 128), F32),
        dma((5,)), dma((4,)), dma((4,)),
        dma, dma, dma, dma,
        dma, dma, dma, dma, dma,
        dma, dma, dma, dma, dma,
    ]
    return pl.pallas_call(
        kernel,
        out_shape=[
            jax.ShapeDtypeStruct(states.shape, F32),
            jax.ShapeDtypeStruct(states.shape, F32),
        ],
        in_specs=[vmem, vmem, anywhere, anywhere, anywhere, vmem, anywhere, anywhere],
        out_specs=[vmem, vmem],
        scratch_shapes=scratch,
        compiler_params=pltpu.CompilerParams(collective_id=0, has_side_effects=True),
    )(states, increments, w_first, w_mid, w_last, biases, cov_x, cov_y)


def solution(mesh):
    block = P("tm", None, "tile", None)
    return jax.shard_map(
        local,
        mesh=mesh,
        in_specs=(block, block, P(), P(), P(), P(), P(), P()),
        out_specs=(block, block),
        check_vma=False,
    )
```

```python
import jax
import jax.numpy as jnp
from jax import lax
from jax.experimental import pallas as pl
from jax.experimental.pallas import tpu as pltpu
from jax.sharding import PartitionSpec as P

F32 = jnp.float32
BF16 = jnp.bfloat16
MESH = pl.DeviceIdType.MESH
TILES = 64
WINDOWS = 4
CHIPS = 32
FAR_FIRST = sorted(
    ((z, x) for z in range(8) for x in range(4) if z or x),
    key=lambda s: -(min(s[0], 8 - s[0]) + min(s[1], 4 - s[1])),
)


def contract(a, b, dims=((1,), (0,))):
    return lax.dot_general(a, b, (dims, ((), ())), preferred_element_type=F32)


def split(x):
    high = x.astype(BF16)
    return high, (x - high.astype(F32)).astype(BF16)


def shifted_rows(v):
    at = lax.broadcasted_iota(jnp.int32, (8, v.shape[1]), 0)
    up = pltpu.roll(v, 1, 0)
    down = pltpu.roll(v, v.shape[0] - 1, 0)
    up = jnp.concatenate([jnp.where(at == 0, 0.0, up[:8]), up[8:]], axis=0)
    down = jnp.concatenate([down[:-8], jnp.where(at == 7, 0.0, down[-8:])], axis=0)
    return up, down


def shifted_lanes(v):
    at = lax.broadcasted_iota(jnp.int32, v.shape, 1)
    n = v.shape[1]
    up = jnp.where(at == 0, 0.0, pltpu.roll(v, 1, 1))
    down = jnp.where(at == n - 1, 0.0, pltpu.roll(v, n - 1, 1))
    return up, down


def put_three(buf, i, v):
    up, down = shifted_rows(v)
    buf[i, :, 0:256] = up.astype(BF16)
    buf[i, :, 256:512] = v.astype(BF16)
    buf[i, :, 512:768] = down.astype(BF16)


def put_taps(buf, i, v):
    up, down = shifted_lanes(v)
    buf[i, 0:16] = up.astype(BF16)
    buf[i, 16:32] = v.astype(BF16)
    buf[i, 32:48] = down.astype(BF16)


def build_thin(dst, tap):
    zero = jnp.zeros((16, 128), BF16)
    for r in range(4):
        for q in range(3):
            for o in range(2):
                p = r - o
                at = (r * 3 + q) * 16
                block = tap(3 * p + q) if 0 <= p <= 2 else zero
                dst[at : at + 16, o * 128 : o * 128 + 128] = block


def build_wide(dst, tap):
    zero = jnp.zeros((128, 128), BF16)
    for pair in range(2):
        for q in range(3):
            for rr in range(2):
                for o in range(2):
                    p = 2 * pair + rr - o
                    at = pair * 768 + q * 256 + rr * 128
                    block = tap(3 * p + q) if 0 <= p <= 2 else zero
                    dst[at : at + 128, o * 128 : o * 128 + 128] = block


def wide_conv(buf, i, weights):
    both = jnp.concatenate([buf[i], buf[i + 1]], axis=1)
    return contract(both, weights[...])


def thin_conv(buf, i, weights):
    return contract(buf[i : i + 4].reshape(192, 256), weights[...], ((0,), (0,)))


def fold_rows(parts, r, flipped):
    sums = []
    for q in range(3):
        total = None
        for p in range(3):
            t = 3 * p + q
            t = 8 - t if flipped else t
            piece = parts[r + p][t * 16 : t * 16 + 16]
            total = piece if total is None else total + piece
        sums.append(total)
    up, _ = shifted_lanes(sums[0])
    _, down = shifted_lanes(sums[2])
    return up + sums[1] + down


def kernel(
    st_h, inc_h, wf_h, wm_h, wl_h, bias_h, cx_h, cy_h,
    high_o, low_o, rest_o,
    st, inc, bias, wf, wm, wl, cx, cy,
    x, xq, tq, a1, t1, a2, t2, t3, b3, b2, b1, s1, s2, s3,
    w1, wk2, wk3, v4, vk3, vk2, cx3, cy3,
    nxt, prev, chg, bx, sbuf, rbuf, obuf, mbuf, high_v, low_v, rest_v,
    insem, wsem, outsem, near, hs, hr, ns, nr, ps, pr, as_, ar, at_s, at_r, al, bs, br, bt_s, bt_r, bl,
):
    tm = lax.axis_index("tm")
    me = lax.axis_index("tile")
    chip = lax.div(me, 2)
    core = lax.rem(me, 2)
    tm_next = lax.rem(tm + 1, WINDOWS)
    tm_back = lax.rem(tm + WINDOWS - 1, WINDOWS)

    def tile_at(step):
        return lax.rem(me + (step + TILES), TILES)

    barrier = pltpu.get_barrier_semaphore()
    for step in (1, -1, 2, -2):
        pl.semaphore_signal(
            barrier, inc=1, device_id={"tile": tile_at(step)}, device_id_type=MESH
        )
    for to in (tm_next, tm_back):
        pl.semaphore_signal(barrier, inc=1, device_id={"tm": to}, device_id_type=MESH)

    takes = [
        pltpu.make_async_copy(src, dst, insem.at[n])
        for n, (src, dst) in enumerate(((st_h, st), (inc_h, inc), (bias_h, bias)))
    ]
    loads = [
        pltpu.make_async_copy(src, dst, wsem.at[n])
        for n, (src, dst) in enumerate(
            ((wf_h, wf), (wm_h, wm), (wl_h, wl), (cx_h, cx), (cy_h, cy))
        )
    ]
    for load in takes + loads:
        load.start()

    def tell(n):
        for step in (2 << n, -(2 << n)):
            pl.semaphore_signal(
                near.at[n], inc=1, device_id={"tile": tile_at(step)}, device_id_type=MESH
            )

    def hear(n):
        pl.semaphore_wait(near.at[n], 2)

    takes[0].wait()
    for r in range(4):
        x[6 + r, 0] = st[0, :, r, :].astype(BF16)
    takes[1].wait()
    for r in range(4):
        x[6 + r, 1] = inc[0, :, r, :].astype(BF16)

    pl.semaphore_wait(barrier, 6)

    halo = []
    for n, (step, src, dst) in enumerate(
        (
            (1, x.at[6:10], x.at[2:6]),
            (TILES - 1, x.at[6:10], x.at[10:14]),
            (2, x.at[8:10, 0], x.at[0:2, 0]),
            (TILES - 2, x.at[6:8, 0], x.at[14:16, 0]),
        )
    ):
        halo.append(
            pltpu.make_async_remote_copy(
                src, dst, hs.at[n], hr.at[n],
                device_id={"tile": lax.rem(me + step, TILES)}, device_id_type=MESH,
            )
        )
    for copy in halo:
        copy.start()
    ahead = pltpu.make_async_remote_copy(
        inc.at[0], nxt, ns, nr, device_id={"tm": tm_back}, device_id_type=MESH
    )
    ahead.start()
    tell(0)

    def valid(e):
        g = 4 * me - 6 + e
        return jnp.where((g >= 0) & (g < 4 * TILES), 1.0, 0.0).astype(F32)

    def pair_mask(e):
        lane = lax.broadcasted_iota(jnp.int32, (1, 256), 1)
        return jnp.where(lane < 128, valid(e), valid(e + 1))

    def inner(e):
        return e >= 6 and e + 1 <= 9

    for e in range(6, 10):
        put_taps(xq, e, x[e, 0].astype(F32))
        put_taps(tq, e, x[e, 1].astype(F32))
    loads[0].wait()
    build_thin(w1, lambda t: wf[t])
    loads[1].wait()
    build_wide(wk2, lambda t: wm[0, t])
    build_wide(wk3, lambda t: wm[1, t])
    loads[2].wait()
    build_thin(v4, lambda t: wl[8 - t])
    loads[3].wait()
    high, low = split(cx[...])
    cx3[:, 0:256] = high
    cx3[:, 256:512] = high
    cx3[:, 512:768] = low
    loads[4].wait()
    high, low = split(cy[...])
    cy3[0:256] = high
    cy3[256:512] = high
    cy3[512:768] = low
    takes[2].wait()
    biases = [jnp.concatenate([bias[l : l + 1], bias[l : l + 1]], axis=1) for l in range(3)]

    hear(0)
    tell(1)
    for copy in halo[:2]:
        copy.wait_recv()

    def edge_row(e, with_tangent):
        put_taps(xq, e, x[e, 0].astype(F32) * valid(e))
        if with_tangent:
            put_taps(tq, e, x[e, 1].astype(F32) * valid(e))

    for e in (2, 3, 4, 5, 10, 11, 12, 13):
        edge_row(e, True)

    def activation(l, z, e, s_buf, i, out):
        h = jnp.tanh(z + biases[l])
        s = 1.0 - h * h
        if not inner(e):
            mask = pair_mask(e)
            s = s * mask
            h = h * mask
        s_buf[i] = s
        if out is not None:
            put_three(out, i, h)
        return s

    def layer_one(i, tangent):
        s = activation(0, thin_conv(xq, 2 * i, w1), 2 * i + 1, s1, i, a1)
        if tangent:
            put_three(t1, i, s * thin_conv(tq, 2 * i, w1))

    def layer_two(i, tangent):
        s = activation(1, wide_conv(a1, i, wk2), 2 * i + 2, s2, i, a2)
        if tangent:
            put_three(t2, i, s * wide_conv(t1, i, wk2))

    def layer_three(i, tangent):
        s = activation(2, wide_conv(a2, i, wk3), 2 * i + 3, s3, i, None)
        if tangent:
            t3[i] = (s * wide_conv(t2, i, wk3)).astype(BF16)

    for i in range(1, 6):
        layer_one(i, True)
    hear(1)
    tell(2)
    for i in range(1, 5):
        layer_two(i, True)
    hear(2)
    tell(3)
    for i in range(1, 4):
        layer_three(i, True)

    last = wl[...].reshape(144, 128)
    parts = []
    for i in range(1, 4):
        for half in range(2):
            parts.append(contract(last, t3[i, :, half * 128 : half * 128 + 128], ((1,), (1,))))
    for r in range(4):
        chg[:, r, :] = fold_rows(parts, r, False)

    ahead.wait_recv()
    not_last = jnp.where(tm == WINDOWS - 1, 0.0, 1.0).astype(F32)
    misfit = nxt[...] * not_last - inc[0] - chg[...]
    high, low = split(misfit.reshape(64, 256))
    smoothed = contract(jnp.concatenate([high, low, high], axis=1), cy3[...])
    for half in range(2):
        sbuf[half * 16 : half * 16 + 16] = smoothed[:, half * 128 : half * 128 + 128].reshape(
            16, 4, 128
        )

    hear(3)

    def chip_at(dz, dx):
        return lax.rem(lax.div(chip, 4) + dz, 8) * 4 + lax.rem(chip + dx, 4)

    def out_chunk(c, send, recv):
        return pltpu.make_async_remote_copy(
            sbuf.at[c], rbuf.at[me], send, recv,
            device_id={"tile": 2 * c}, device_id_type=MESH,
        )

    for dz, dx in FAR_FIRST:
        out_chunk(chip_at(dz, dx), as_, ar).start()
    own_chunk = pltpu.make_async_copy(sbuf.at[chip], rbuf.at[me], al)

    @pl.when(core == 0)
    def _():
        own_chunk.start()

    @pl.when(core == 1)
    def _():
        out_chunk(chip, at_s, at_r).start()

    for copy in halo[2:]:
        copy.wait_recv()
    for e in (0, 1, 14, 15):
        edge_row(e, False)
    for i in (0, 6):
        layer_one(i, False)
    for i in (0, 5):
        layer_two(i, False)
    for i in (0, 4):
        layer_three(i, False)
    build_wide(vk3, lambda t: wm[1, 8 - t].T)
    build_wide(vk2, lambda t: wm[0, 8 - t].T)

    @pl.when(core == 0)
    def _():
        obuf[0, 0] = jnp.zeros((4, 128), BF16)
        obuf[TILES - 1, 1] = jnp.zeros((4, 128), BF16)
        own_chunk.wait()
        partner = pltpu.make_async_remote_copy(
            sbuf.at[0], rbuf.at[me + 1], at_s, at_r,
            device_id={"tile": me}, device_id_type=MESH,
        )
        partner.wait_recv()
        pltpu.make_async_copy(
            rbuf.at[0 : TILES - 2], rbuf.at[0 : TILES - 2], ar
        ).wait()
        high, low = split(rbuf[...].reshape(256, 128))
        result = contract(cx3[...], jnp.concatenate([high, low, high], axis=0))
        high, low = split(result)
        high = high.reshape(TILES, 4, 128)
        obuf[1:TILES, 0] = high[0 : TILES - 1]
        obuf[0 : TILES - 1, 1] = high[1:TILES]
        obuf[:, 2] = high
        obuf[:, 3] = low.reshape(TILES, 4, 128)

        def back_chunk(d, send, recv):
            return pltpu.make_async_remote_copy(
                obuf.at[d], mbuf.at[chip], send, recv,
                device_id={"tile": d}, device_id_type=MESH,
            )

        for dz, dx in FAR_FIRST:
            c = chip_at(dz, dx)
            for half in range(2):
                back_chunk(2 * c + half, bs, br).start()
        back_chunk(me + 1, bt_s, bt_r).start()
        own_back = pltpu.make_async_copy(obuf.at[me], mbuf.at[chip], bl)
        own_back.start()
        own_back.wait()

    @pl.when(core == 1)
    def _():
        pltpu.make_async_remote_copy(
            obuf.at[0], mbuf.at[chip], bt_s, bt_r,
            device_id={"tile": me}, device_id_type=MESH,
        ).wait_recv()

    pltpu.make_async_copy(mbuf.at[0 : CHIPS - 1], mbuf.at[0 : CHIPS - 1], br).wait()

    behind = pltpu.make_async_remote_copy(
        mbuf.at[:, 2:4], prev, ps, pr, device_id={"tm": tm_next}, device_id_type=MESH
    )
    behind.start()

    for half in range(2):
        lanes = slice(half * 128, half * 128 + 128)
        chunk = slice(half * 16, half * 16 + 16)
        for j, slot in enumerate((0, 2, 1)):
            bx[j, :, :, lanes] = mbuf[chunk, slot].astype(F32)
        high_v[0, :, :, lanes] = mbuf[chunk, 2]
        low_v[0, :, :, lanes] = mbuf[chunk, 3]
    outs = [
        pltpu.make_async_copy(src, dst, outsem.at[n])
        for n, (src, dst) in enumerate(((high_v, high_o), (low_v, low_o), (rest_v, rest_o)))
    ]
    outs[0].start()
    outs[1].start()

    for idx in range(12):
        j, k = idx // 4, idx % 4
        row = bx[j, :, k, :]
        if j != 1:
            row = row * valid(2 + idx)
        put_taps(xq, idx, row)
    for i in range(5):
        b = s3[i] * thin_conv(xq, 2 * i, v4)
        put_three(b3, i, b)
    for i in range(4):
        put_three(b2, i, s2[i + 1] * wide_conv(b3, i, vk3))
    for i in range(3):
        b1[i] = (s1[i + 2] * wide_conv(b2, i, vk2)).astype(BF16)
    first = wf[...].reshape(144, 128)
    parts = []
    for i in range(3):
        for half in range(2):
            parts.append(contract(first, b1[i, :, half * 128 : half * 128 + 128], ((1,), (1,))))
    for r in range(4):
        chg[:, r, :] = fold_rows(parts, r, True)

    behind.wait_recv()
    not_first = jnp.where(tm == 0, 0.0, 1.0).astype(F32)
    for half in range(2):
        lanes = slice(half * 128, half * 128 + 128)
        chunk = slice(half * 16, half * 16 + 16)
        earlier = prev[chunk, 0].astype(F32) + prev[chunk, 1].astype(F32)
        rest_v[0, :, :, lanes] = earlier * not_first - chg[:, :, lanes]
    outs[2].start()

    for copy in halo:
        copy.wait_send()
    ahead.wait_send()
    behind.wait_send()
    pltpu.make_async_copy(sbuf.at[0 : CHIPS - 1], sbuf.at[0 : CHIPS - 1], as_).wait()

    @pl.when(core == 1)
    def _():
        pltpu.make_async_copy(sbuf.at[0], sbuf.at[0], at_s).wait()

    @pl.when(core == 0)
    def _():
        pltpu.make_async_copy(obuf.at[0], obuf.at[0], bt_s).wait()
        sent = mbuf.at[0 : CHIPS - 1]
        pltpu.make_async_copy(sent, sent, bs).wait()
        pltpu.make_async_copy(sent, sent, bs).wait()

    for out in outs:
        out.wait()


def local(states, increments, w_first, w_mid, w_last, biases, cov_x, cov_y):
    anywhere = pl.BlockSpec(memory_space=pl.ANY)
    dma = pltpu.SemaphoreType.DMA
    scratch = [
        pltpu.VMEM((1, 16, 4, 256), F32),
        pltpu.VMEM((1, 16, 4, 256), F32),
        pltpu.VMEM((3, 128), F32),
        pltpu.VMEM((9, 16, 128), BF16),
        pltpu.VMEM((2, 9, 128, 128), BF16),
        pltpu.VMEM((9, 16, 128), BF16),
        pltpu.VMEM((256, 256), F32),
        pltpu.VMEM((256, 256), F32),
        pltpu.VMEM((16, 2, 16, 256), BF16),
        pltpu.VMEM((16, 48, 256), BF16),
        pltpu.VMEM((16, 48, 256), BF16),
        pltpu.VMEM((7, 256, 768), BF16),
        pltpu.VMEM((7, 256, 768), BF16),
        pltpu.VMEM((6, 256, 768), BF16),
        pltpu.VMEM((6, 256, 768), BF16),
        pltpu.VMEM((5, 256, 256), BF16),
        pltpu.VMEM((5, 256, 768), BF16),
        pltpu.VMEM((4, 256, 768), BF16),
        pltpu.VMEM((3, 256, 256), BF16),
        pltpu.VMEM((7, 256, 256), F32),
        pltpu.VMEM((6, 256, 256), F32),
        pltpu.VMEM((5, 256, 256), F32),
        pltpu.VMEM((192, 256), BF16),
        pltpu.VMEM((1536, 256), BF16),
        pltpu.VMEM((1536, 256), BF16),
        pltpu.VMEM((192, 256), BF16),
        pltpu.VMEM((1536, 256), BF16),
        pltpu.VMEM((1536, 256), BF16),
        pltpu.VMEM((256, 768), BF16),
        pltpu.VMEM((768, 256), BF16),
        pltpu.VMEM((16, 4, 256), F32),
        pltpu.VMEM((32, 2, 4, 128), BF16),
        pltpu.VMEM((16, 4, 256), F32),
        pltpu.VMEM((3, 16, 4, 256), F32),
        pltpu.VMEM((32, 4, 128), F32),
        pltpu.VMEM((TILES, 4, 128), F32),
        pltpu.VMEM((TILES, 4, 4, 128), BF16),
        pltpu.VMEM((32, 4, 4, 128), BF16),
        pltpu.VMEM((1, 16, 4, 256), BF16),
        pltpu.VMEM((1, 16, 4, 256), BF16),
        pltpu.VMEM((1, 16, 4, 256), F32),
        dma((3,)), dma((5,)), dma((3,)), pltpu.SemaphoreType.REGULAR((4,)),
        dma((4,)), dma((4,)),
        dma, dma, dma, dma,
        dma, dma, dma, dma, dma,
        dma, dma, dma, dma, dma,
    ]
    high, low, rest = pl.pallas_call(
        kernel,
        out_shape=[
            jax.ShapeDtypeStruct(states.shape, BF16),
            jax.ShapeDtypeStruct(states.shape, BF16),
            jax.ShapeDtypeStruct(states.shape, F32),
        ],
        in_specs=[anywhere] * 8,
        out_specs=[anywhere] * 3,
        scratch_shapes=scratch,
        compiler_params=pltpu.CompilerParams(collective_id=0, has_side_effects=True),
    )(states, increments, w_first, w_mid, w_last, biases, cov_x, cov_y)
    multiplier = high.astype(F32) + low.astype(F32)
    return multiplier, rest - multiplier


def solution(mesh):
    block = P("tm", None, "tile", None)
    return jax.shard_map(
        local,
        mesh=mesh,
        in_specs=(block, block, P(), P(), P(), P(), P(), P()),
        out_specs=(block, block),
        check_vma=False,
    )
```

```python
import jax
import jax.numpy as jnp
from jax import lax
from jax.experimental import pallas as pl
from jax.experimental.pallas import tpu as pltpu
from jax.sharding import PartitionSpec as P

F32 = jnp.float32
BF16 = jnp.bfloat16
MESH = pl.DeviceIdType.MESH
TILES = 64
WINDOWS = 4
CHIPS = 32
FAR_FIRST = sorted(
    ((z, x) for z in range(8) for x in range(4) if z or x),
    key=lambda s: -(min(s[0], 8 - s[0]) + min(s[1], 4 - s[1])),
)


def contract(a, b, dims=((1,), (0,))):
    return lax.dot_general(a, b, (dims, ((), ())), preferred_element_type=F32)


def split(x):
    high = x.astype(BF16)
    return high, (x - high.astype(F32)).astype(BF16)


def shifted_rows(v):
    at = lax.broadcasted_iota(jnp.int32, (8, v.shape[1]), 0)
    up = pltpu.roll(v, 1, 0)
    down = pltpu.roll(v, v.shape[0] - 1, 0)
    up = jnp.concatenate([jnp.where(at == 0, 0.0, up[:8]), up[8:]], axis=0)
    down = jnp.concatenate([down[:-8], jnp.where(at == 7, 0.0, down[-8:])], axis=0)
    return up, down


def shifted_lanes(v):
    at = lax.broadcasted_iota(jnp.int32, v.shape, 1)
    n = v.shape[1]
    up = jnp.where(at == 0, 0.0, pltpu.roll(v, 1, 1))
    down = jnp.where(at == n - 1, 0.0, pltpu.roll(v, n - 1, 1))
    return up, down


def put_three(buf, i, v):
    up, down = shifted_rows(v)
    buf[i, :, 0:256] = up.astype(BF16)
    buf[i, :, 256:512] = v.astype(BF16)
    buf[i, :, 512:768] = down.astype(BF16)


def put_taps(buf, i, v):
    up, down = shifted_lanes(v)
    buf[i, 0:16] = up.astype(BF16)
    buf[i, 16:32] = v.astype(BF16)
    buf[i, 32:48] = down.astype(BF16)


def build_thin(dst, tap):
    zero = jnp.zeros((16, 128), BF16)
    for r in range(4):
        for q in range(3):
            for o in range(2):
                p = r - o
                at = (r * 3 + q) * 16
                block = tap(3 * p + q) if 0 <= p <= 2 else zero
                dst[at : at + 16, o * 128 : o * 128 + 128] = block


def build_wide(dst, tap):
    zero = jnp.zeros((128, 128), BF16)
    for pair in range(2):
        for q in range(3):
            for rr in range(2):
                for o in range(2):
                    p = 2 * pair + rr - o
                    at = pair * 768 + q * 256 + rr * 128
                    block = tap(3 * p + q) if 0 <= p <= 2 else zero
                    dst[at : at + 128, o * 128 : o * 128 + 128] = block


def wide_conv(buf, i, weights):
    both = jnp.concatenate([buf[i], buf[i + 1]], axis=1)
    return contract(both, weights[...])


def thin_conv(buf, i, weights):
    return contract(buf[i : i + 4].reshape(192, 256), weights[...], ((0,), (0,)))


def fold_rows(parts, r, flipped):
    sums = []
    for q in range(3):
        total = None
        for p in range(3):
            t = 3 * p + q
            t = 8 - t if flipped else t
            piece = parts[r + p][t * 16 : t * 16 + 16]
            total = piece if total is None else total + piece
        sums.append(total)
    up, _ = shifted_lanes(sums[0])
    _, down = shifted_lanes(sums[2])
    return up + sums[1] + down


def kernel(
    st_h, inc_h, wf_h, wm_h, wl_h, bias_h, cx_h, cy_h,
    high_o, low_o, rest_o,
    st, inc, bias, wf, wm, wl, cx, cy,
    x, xq, tq, a1, t1, a2, t2, t3, b3, b2, b1, s1, s2, s3,
    w1, wk2, wk3, v4, vk3, vk2, cx3, cy3,
    nxt, prev, chg, bx, sbuf, rbuf, obuf, mbuf,
    insem, wsem, near, hs, hr, ns, nr, ps, pr, as_, ar, at_s, at_r, al, bs, br, bt_s, bt_r, bl,
):
    tm = lax.axis_index("tm")
    me = lax.axis_index("tile")
    chip = lax.div(me, 2)
    core = lax.rem(me, 2)
    has_next = tm < WINDOWS - 1
    has_back = tm > 0
    tm_next = jnp.minimum(tm + 1, WINDOWS - 1)
    tm_back = jnp.maximum(tm - 1, 0)

    def tile_at(step):
        return lax.rem(me + (step + TILES), TILES)

    barrier = pltpu.get_barrier_semaphore()
    for step in (1, -1, 2, -2):
        pl.semaphore_signal(
            barrier, inc=1, device_id={"tile": tile_at(step)}, device_id_type=MESH
        )

    @pl.when(has_next)
    def _():
        pl.semaphore_signal(
            barrier, inc=1, device_id={"tm": tm_next}, device_id_type=MESH
        )

    takes = [
        pltpu.make_async_copy(src, dst, insem.at[n])
        for n, (src, dst) in enumerate(((st_h, st), (inc_h, inc), (bias_h, bias)))
    ]
    loads = [
        pltpu.make_async_copy(src, dst, wsem.at[n])
        for n, (src, dst) in enumerate(
            ((wf_h, wf), (wm_h, wm), (wl_h, wl), (cx_h, cx), (cy_h, cy))
        )
    ]
    for load in takes + loads:
        load.start()

    def tell(n):
        for step in (2 << n, -(2 << n)):
            pl.semaphore_signal(
                near.at[n], inc=1, device_id={"tile": tile_at(step)}, device_id_type=MESH
            )

    def hear(n):
        pl.semaphore_wait(near.at[n], 2)

    takes[0].wait()
    for r in range(4):
        x[6 + r, 0] = st[0, :, r, :].astype(BF16)
    takes[1].wait()
    for r in range(4):
        x[6 + r, 1] = inc[0, :, r, :].astype(BF16)

    pl.semaphore_wait(barrier, jnp.where(has_back, 5, 4))

    halo = []
    for n, (step, src, dst) in enumerate(
        (
            (1, x.at[6:10], x.at[2:6]),
            (TILES - 1, x.at[6:10], x.at[10:14]),
            (2, x.at[8:10, 0], x.at[0:2, 0]),
            (TILES - 2, x.at[6:8, 0], x.at[14:16, 0]),
        )
    ):
        halo.append(
            pltpu.make_async_remote_copy(
                src, dst, hs.at[n], hr.at[n],
                device_id={"tile": lax.rem(me + step, TILES)}, device_id_type=MESH,
            )
        )
    for copy in halo:
        copy.start()
    ahead = pltpu.make_async_remote_copy(
        inc.at[0], nxt, ns, nr, device_id={"tm": tm_back}, device_id_type=MESH
    )
    tell(0)

    @pl.when(has_back)
    def _():
        ahead.start()


    def valid(e):
        g = 4 * me - 6 + e
        return jnp.where((g >= 0) & (g < 4 * TILES), 1.0, 0.0).astype(F32)

    def pair_mask(e):
        lane = lax.broadcasted_iota(jnp.int32, (1, 256), 1)
        return jnp.where(lane < 128, valid(e), valid(e + 1))

    def inner(e):
        return e >= 6 and e + 1 <= 9

    for e in range(6, 10):
        put_taps(xq, e, x[e, 0].astype(F32))
        put_taps(tq, e, x[e, 1].astype(F32))
    loads[0].wait()
    build_thin(w1, lambda t: wf[t])
    hear(0)
    tell(1)
    loads[1].wait()
    build_wide(wk2, lambda t: wm[0, t])
    build_wide(wk3, lambda t: wm[1, t])
    loads[2].wait()
    build_thin(v4, lambda t: wl[8 - t])
    loads[3].wait()
    high, low = split(cx[...])
    cx3[:, 0:256] = high
    cx3[:, 256:512] = high
    cx3[:, 512:768] = low
    loads[4].wait()
    high, low = split(cy[...])
    cy3[0:256] = high
    cy3[256:512] = high
    cy3[512:768] = low
    takes[2].wait()
    hear(1)
    tell(2)
    biases = [jnp.concatenate([bias[l : l + 1], bias[l : l + 1]], axis=1) for l in range(3)]

    def edge_row(e, with_tangent):
        put_taps(xq, e, x[e, 0].astype(F32) * valid(e))
        if with_tangent:
            put_taps(tq, e, x[e, 1].astype(F32) * valid(e))

    def activation(l, z, e, s_buf, i, out):
        h = jnp.tanh(z + biases[l])
        s = 1.0 - h * h
        if not inner(e):
            mask = pair_mask(e)
            s = s * mask
            h = h * mask
        s_buf[i] = s
        if out is not None:
            put_three(out, i, h)
        return s

    def layer_one(i, tangent):
        s = activation(0, thin_conv(xq, 2 * i, w1), 2 * i + 1, s1, i, a1)
        if tangent:
            put_three(t1, i, s * thin_conv(tq, 2 * i, w1))

    def layer_two(i, tangent):
        s = activation(1, wide_conv(a1, i, wk2), 2 * i + 2, s2, i, a2)
        if tangent:
            put_three(t2, i, s * wide_conv(t1, i, wk2))

    def layer_three(i, tangent):
        s = activation(2, wide_conv(a2, i, wk3), 2 * i + 3, s3, i, None)
        if tangent:
            t3[i] = (s * wide_conv(t2, i, wk3)).astype(BF16)

    layer_one(3, True)
    for copy in halo[:2]:
        copy.wait_recv()

    for e in (2, 3, 4, 5, 10, 11, 12, 13):
        edge_row(e, True)
    for i in (1, 2, 4, 5):
        layer_one(i, True)
    hear(2)
    tell(3)
    for i in range(1, 5):
        layer_two(i, True)
    for i in range(1, 4):
        layer_three(i, True)

    last = wl[...].reshape(144, 128)
    parts = []
    for i in range(1, 4):
        for half in range(2):
            parts.append(contract(last, t3[i, :, half * 128 : half * 128 + 128], ((1,), (1,))))
    for r in range(4):
        chg[:, r, :] = fold_rows(parts, r, False)

    @pl.when(has_next)
    def _():
        ahead.wait_recv()

    @pl.when(tm == WINDOWS - 1)
    def _():
        nxt[...] = jnp.zeros(nxt.shape, F32)

    misfit = nxt[...] - inc[0] - chg[...]
    high, low = split(misfit.reshape(64, 256))
    smoothed = contract(jnp.concatenate([high, low, high], axis=1), cy3[...])
    for half in range(2):
        sbuf[half * 16 : half * 16 + 16] = smoothed[:, half * 128 : half * 128 + 128].reshape(
            16, 4, 128
        )

    hear(3)

    def chip_at(dz, dx):
        return lax.rem(lax.div(chip, 4) + dz, 8) * 4 + lax.rem(chip + dx, 4)

    def out_chunk(c, send, recv):
        return pltpu.make_async_remote_copy(
            sbuf.at[c], rbuf.at[me], send, recv,
            device_id={"tile": 2 * c}, device_id_type=MESH,
        )

    for dz, dx in FAR_FIRST:
        out_chunk(chip_at(dz, dx), as_, ar).start()
    own_chunk = pltpu.make_async_copy(sbuf.at[chip], rbuf.at[me], al)

    @pl.when(core == 0)
    def _():
        own_chunk.start()

    @pl.when(core == 1)
    def _():
        out_chunk(chip, at_s, at_r).start()

    for copy in halo[2:]:
        copy.wait_recv()
    for e in (0, 1, 14, 15):
        edge_row(e, False)
    for i in (0, 6):
        layer_one(i, False)
    for i in (0, 5):
        layer_two(i, False)
    for i in (0, 4):
        layer_three(i, False)
    build_wide(vk3, lambda t: wm[1, 8 - t].T)
    build_wide(vk2, lambda t: wm[0, 8 - t].T)

    @pl.when(core == 0)
    def _():
        obuf[0, 0] = jnp.zeros((4, 128), BF16)
        obuf[TILES - 1, 1] = jnp.zeros((4, 128), BF16)
        own_chunk.wait()
        partner = pltpu.make_async_remote_copy(
            sbuf.at[0], rbuf.at[me + 1], at_s, at_r,
            device_id={"tile": me}, device_id_type=MESH,
        )
        partner.wait_recv()
        pltpu.make_async_copy(
            rbuf.at[0 : TILES - 2], rbuf.at[0 : TILES - 2], ar
        ).wait()
        high, low = split(rbuf[...].reshape(256, 128))
        result = contract(cx3[...], jnp.concatenate([high, low, high], axis=0))
        high, low = split(result)
        high = high.reshape(TILES, 4, 128)
        obuf[1:TILES, 0] = high[0 : TILES - 1]
        obuf[0 : TILES - 1, 1] = high[1:TILES]
        obuf[:, 2] = high
        obuf[:, 3] = low.reshape(TILES, 4, 128)

        def back_chunk(d, send, recv):
            return pltpu.make_async_remote_copy(
                obuf.at[d], mbuf.at[chip], send, recv,
                device_id={"tile": d}, device_id_type=MESH,
            )

        for dz, dx in FAR_FIRST:
            c = chip_at(dz, dx)
            for half in range(2):
                back_chunk(2 * c + half, bs, br).start()
        back_chunk(me + 1, bt_s, bt_r).start()
        own_back = pltpu.make_async_copy(obuf.at[me], mbuf.at[chip], bl)
        own_back.start()
        own_back.wait()

    @pl.when(core == 1)
    def _():
        pltpu.make_async_remote_copy(
            obuf.at[0], mbuf.at[chip], bt_s, bt_r,
            device_id={"tile": me}, device_id_type=MESH,
        ).wait_recv()

    pltpu.make_async_copy(mbuf.at[0 : CHIPS - 1], mbuf.at[0 : CHIPS - 1], br).wait()

    behind = pltpu.make_async_remote_copy(
        mbuf.at[:, 2:4], prev, ps, pr, device_id={"tm": tm_next}, device_id_type=MESH
    )

    @pl.when(has_next)
    def _():
        behind.start()


    for half in range(2):
        lanes = slice(half * 128, half * 128 + 128)
        chunk = slice(half * 16, half * 16 + 16)
        for j, slot in enumerate((0, 2, 1)):
            bx[j, :, :, lanes] = mbuf[chunk, slot].astype(F32)
        high_o[0, :, :, lanes] = mbuf[chunk, 2]
        low_o[0, :, :, lanes] = mbuf[chunk, 3]

    for idx in range(12):
        j, k = idx // 4, idx % 4
        row = bx[j, :, k, :]
        if j != 1:
            row = row * valid(2 + idx)
        put_taps(xq, idx, row)
    for i in range(5):
        b = s3[i] * thin_conv(xq, 2 * i, v4)
        put_three(b3, i, b)
    for i in range(4):
        put_three(b2, i, s2[i + 1] * wide_conv(b3, i, vk3))
    for i in range(3):
        b1[i] = (s1[i + 2] * wide_conv(b2, i, vk2)).astype(BF16)
    first = wf[...].reshape(144, 128)
    parts = []
    for i in range(3):
        for half in range(2):
            parts.append(contract(first, b1[i, :, half * 128 : half * 128 + 128], ((1,), (1,))))
    for r in range(4):
        chg[:, r, :] = fold_rows(parts, r, True)

    @pl.when(has_back)
    def _():
        behind.wait_recv()

    @pl.when(tm == 0)
    def _():
        prev[...] = jnp.zeros(prev.shape, BF16)

    for half in range(2):
        lanes = slice(half * 128, half * 128 + 128)
        chunk = slice(half * 16, half * 16 + 16)
        earlier = prev[chunk, 0].astype(F32) + prev[chunk, 1].astype(F32)
        rest_o[0, :, :, lanes] = earlier - chg[:, :, lanes]

    for copy in halo:
        copy.wait_send()

    @pl.when(has_back)
    def _():
        ahead.wait_send()

    @pl.when(has_next)
    def _():
        behind.wait_send()

    pltpu.make_async_copy(sbuf.at[0 : CHIPS - 1], sbuf.at[0 : CHIPS - 1], as_).wait()

    @pl.when(core == 1)
    def _():
        pltpu.make_async_copy(sbuf.at[0], sbuf.at[0], at_s).wait()

    @pl.when(core == 0)
    def _():
        pltpu.make_async_copy(obuf.at[0], obuf.at[0], bt_s).wait()
        sent = mbuf.at[0 : CHIPS - 1]
        pltpu.make_async_copy(sent, sent, bs).wait()
        pltpu.make_async_copy(sent, sent, bs).wait()


def local(states, increments, w_first, w_mid, w_last, biases, cov_x, cov_y):
    anywhere = pl.BlockSpec(memory_space=pl.ANY)
    dma = pltpu.SemaphoreType.DMA
    scratch = [
        pltpu.VMEM((1, 16, 4, 256), F32),
        pltpu.VMEM((1, 16, 4, 256), F32),
        pltpu.VMEM((3, 128), F32),
        pltpu.VMEM((9, 16, 128), BF16),
        pltpu.VMEM((2, 9, 128, 128), BF16),
        pltpu.VMEM((9, 16, 128), BF16),
        pltpu.VMEM((256, 256), F32),
        pltpu.VMEM((256, 256), F32),
        pltpu.VMEM((16, 2, 16, 256), BF16),
        pltpu.VMEM((16, 48, 256), BF16),
        pltpu.VMEM((16, 48, 256), BF16),
        pltpu.VMEM((7, 256, 768), BF16),
        pltpu.VMEM((7, 256, 768), BF16),
        pltpu.VMEM((6, 256, 768), BF16),
        pltpu.VMEM((6, 256, 768), BF16),
        pltpu.VMEM((5, 256, 256), BF16),
        pltpu.VMEM((5, 256, 768), BF16),
        pltpu.VMEM((4, 256, 768), BF16),
        pltpu.VMEM((3, 256, 256), BF16),
        pltpu.VMEM((7, 256, 256), F32),
        pltpu.VMEM((6, 256, 256), F32),
        pltpu.VMEM((5, 256, 256), F32),
        pltpu.VMEM((192, 256), BF16),
        pltpu.VMEM((1536, 256), BF16),
        pltpu.VMEM((1536, 256), BF16),
        pltpu.VMEM((192, 256), BF16),
        pltpu.VMEM((1536, 256), BF16),
        pltpu.VMEM((1536, 256), BF16),
        pltpu.VMEM((256, 768), BF16),
        pltpu.VMEM((768, 256), BF16),
        pltpu.VMEM((16, 4, 256), F32),
        pltpu.VMEM((32, 2, 4, 128), BF16),
        pltpu.VMEM((16, 4, 256), F32),
        pltpu.VMEM((3, 16, 4, 256), F32),
        pltpu.VMEM((32, 4, 128), F32),
        pltpu.VMEM((TILES, 4, 128), F32),
        pltpu.VMEM((TILES, 4, 4, 128), BF16),
        pltpu.VMEM((32, 4, 4, 128), BF16),
        dma((3,)), dma((5,)), pltpu.SemaphoreType.REGULAR((4,)),
        dma((4,)), dma((4,)),
        dma, dma, dma, dma,
        dma, dma, dma, dma, dma,
        dma, dma, dma, dma, dma,
    ]
    high, low, rest = pl.pallas_call(
        kernel,
        out_shape=[
            pltpu.VMEM(states.shape, BF16),
            pltpu.VMEM(states.shape, BF16),
            pltpu.VMEM(states.shape, F32),
        ],
        in_specs=[anywhere] * 8,
        out_specs=[pl.BlockSpec(memory_space=pltpu.VMEM)] * 3,
        scratch_shapes=scratch,
        compiler_params=pltpu.CompilerParams(collective_id=0, has_side_effects=True),
    )(states, increments, w_first, w_mid, w_last, biases, cov_x, cov_y)
    multiplier = high.astype(F32) + low.astype(F32)
    return multiplier, rest - multiplier


def solution(mesh):
    block = P("tm", None, "tile", None)
    return jax.shard_map(
        local,
        mesh=mesh,
        in_specs=(block, block, P(), P(), P(), P(), P(), P()),
        out_specs=(block, block),
        check_vma=False,
    )
```

```python
import jax
import jax.numpy as jnp
from jax import lax
from jax.experimental import pallas as pl
from jax.experimental.pallas import tpu as pltpu
from jax.sharding import PartitionSpec as P

F32 = jnp.float32
BF16 = jnp.bfloat16
MESH = pl.DeviceIdType.MESH
TILES = 64
WINDOWS = 4
CHIPS = 32
FAR_FIRST = sorted(
    ((z, x) for z in range(8) for x in range(4) if z or x),
    key=lambda s: -(min(s[0], 8 - s[0]) + min(s[1], 4 - s[1])),
)


def contract(a, b, dims=((1,), (0,))):
    return lax.dot_general(a, b, (dims, ((), ())), preferred_element_type=F32)


def split(x):
    high = x.astype(BF16)
    return high, (x - high.astype(F32)).astype(BF16)


def shifted_rows(v):
    at = lax.broadcasted_iota(jnp.int32, (8, v.shape[1]), 0)
    up = pltpu.roll(v, 1, 0)
    down = pltpu.roll(v, v.shape[0] - 1, 0)
    up = jnp.concatenate([jnp.where(at == 0, 0.0, up[:8]), up[8:]], axis=0)
    down = jnp.concatenate([down[:-8], jnp.where(at == 7, 0.0, down[-8:])], axis=0)
    return up, down


def shifted_lanes(v):
    at = lax.broadcasted_iota(jnp.int32, v.shape, 1)
    n = v.shape[1]
    up = jnp.where(at == 0, 0.0, pltpu.roll(v, 1, 1))
    down = jnp.where(at == n - 1, 0.0, pltpu.roll(v, n - 1, 1))
    return up, down


def put_three(buf, i, v):
    up, down = shifted_rows(v)
    buf[i, :, 0:256] = up.astype(BF16)
    buf[i, :, 256:512] = v.astype(BF16)
    buf[i, :, 512:768] = down.astype(BF16)


def put_taps(buf, i, v):
    up, down = shifted_lanes(v)
    buf[i, 0:16] = up.astype(BF16)
    buf[i, 16:32] = v.astype(BF16)
    buf[i, 32:48] = down.astype(BF16)


def build_thin(dst, tap):
    zero = jnp.zeros((16, 128), BF16)
    for r in range(4):
        for q in range(3):
            for o in range(2):
                p = r - o
                at = (r * 3 + q) * 16
                block = tap(3 * p + q) if 0 <= p <= 2 else zero
                dst[at : at + 16, o * 128 : o * 128 + 128] = block


def build_wide(dst, tap):
    zero = jnp.zeros((128, 128), BF16)
    for pair in range(2):
        for q in range(3):
            for rr in range(2):
                for o in range(2):
                    p = 2 * pair + rr - o
                    at = pair * 768 + q * 256 + rr * 128
                    block = tap(3 * p + q) if 0 <= p <= 2 else zero
                    dst[at : at + 128, o * 128 : o * 128 + 128] = block


def wide_conv(buf, i, weights):
    both = jnp.concatenate([buf[i], buf[i + 1]], axis=1)
    return contract(both, weights[...])


def thin_conv(buf, i, weights):
    return contract(buf[i : i + 4].reshape(192, 256), weights[...], ((0,), (0,)))


def fold_rows(parts, r, flipped):
    sums = []
    for q in range(3):
        total = None
        for p in range(3):
            t = 3 * p + q
            t = 8 - t if flipped else t
            piece = parts[r + p][t * 16 : t * 16 + 16]
            total = piece if total is None else total + piece
        sums.append(total)
    up, _ = shifted_lanes(sums[0])
    _, down = shifted_lanes(sums[2])
    return up + sums[1] + down


def kernel(
    st_h, inc_h, wf_h, wm_h, wl_h, bias_h, cx_h, cy_h,
    high_o, low_o, rest_o,
    st, inc, bias, wf, wm, wl, cx, cy,
    x, xq, tq, a1, t1, a2, t2, t3, b3, b2, b1, s1, s2, s3,
    w1, wk2, wk3, v4, vk3, vk2, cx3, cy3,
    nxt, prev, chg, bx, sbuf, rbuf, obuf, mbuf,
    insem, wsem, near, hs, hr, ns, nr, ps, pr, as_, ar, at_s, at_r, al, bs, br, bt_s, bt_r, bl,
):
    tm = lax.axis_index("tm")
    me = lax.axis_index("tile")
    chip = lax.div(me, 2)
    core = lax.rem(me, 2)
    has_next = tm < WINDOWS - 1
    has_back = tm > 0
    tm_next = jnp.minimum(tm + 1, WINDOWS - 1)
    tm_back = jnp.maximum(tm - 1, 0)

    def tile_at(step):
        return lax.rem(me + (step + TILES), TILES)

    barrier = pltpu.get_barrier_semaphore()
    def greet(to):
        pl.semaphore_signal(barrier, inc=1, device_id={"tile": to}, device_id_type=MESH)

    for step in (1, -1, 2, -2, 8, -8, 16, -16):
        greet(tile_at(step))
    for step in range(1, 8):
        greet(lax.div(me, 8) * 8 + lax.rem(me + step, 8))

    @pl.when(has_next)
    def _():
        pl.semaphore_signal(
            barrier, inc=1, device_id={"tm": tm_next}, device_id_type=MESH
        )

    takes = [
        pltpu.make_async_copy(src, dst, insem.at[n])
        for n, (src, dst) in enumerate(((st_h, st), (inc_h, inc), (bias_h, bias)))
    ]
    loads = [
        pltpu.make_async_copy(src, dst, wsem.at[n])
        for n, (src, dst) in enumerate(
            ((wf_h, wf), (wm_h, wm), (wl_h, wl), (cx_h, cx), (cy_h, cy))
        )
    ]
    for load in takes + loads:
        load.start()

    def tell(n):
        for step in (8, -8, 16, -16):
            pl.semaphore_signal(
                near.at[n], inc=1, device_id={"tile": tile_at(step)}, device_id_type=MESH
            )

    def hear(n):
        pl.semaphore_wait(near.at[n], 4)

    takes[0].wait()
    for r in range(4):
        x[6 + r, 0] = st[0, :, r, :].astype(BF16)
    takes[1].wait()
    for r in range(4):
        x[6 + r, 1] = inc[0, :, r, :].astype(BF16)

    pl.semaphore_wait(barrier, jnp.where(has_back, 16, 15))

    halo = []
    for n, (step, src, dst) in enumerate(
        (
            (1, x.at[6:10], x.at[2:6]),
            (TILES - 1, x.at[6:10], x.at[10:14]),
            (2, x.at[8:10, 0], x.at[0:2, 0]),
            (TILES - 2, x.at[6:8, 0], x.at[14:16, 0]),
        )
    ):
        halo.append(
            pltpu.make_async_remote_copy(
                src, dst, hs.at[n], hr.at[n],
                device_id={"tile": lax.rem(me + step, TILES)}, device_id_type=MESH,
            )
        )
    for copy in halo:
        copy.start()
    ahead = pltpu.make_async_remote_copy(
        inc.at[0], nxt, ns, nr, device_id={"tm": tm_back}, device_id_type=MESH
    )
    tell(0)

    @pl.when(has_back)
    def _():
        ahead.start()


    def valid(e):
        g = 4 * me - 6 + e
        return jnp.where((g >= 0) & (g < 4 * TILES), 1.0, 0.0).astype(F32)

    def pair_mask(e):
        lane = lax.broadcasted_iota(jnp.int32, (1, 256), 1)
        return jnp.where(lane < 128, valid(e), valid(e + 1))

    def inner(e):
        return e >= 6 and e + 1 <= 9

    for e in range(6, 10):
        put_taps(xq, e, x[e, 0].astype(F32))
        put_taps(tq, e, x[e, 1].astype(F32))
    loads[0].wait()
    build_thin(w1, lambda t: wf[t])
    hear(0)
    tell(1)
    loads[1].wait()
    build_wide(wk2, lambda t: wm[0, t])
    build_wide(wk3, lambda t: wm[1, t])
    loads[2].wait()
    build_thin(v4, lambda t: wl[8 - t])
    loads[3].wait()
    high, low = split(cx[...])
    cx3[:, 0:256] = high
    cx3[:, 256:512] = high
    cx3[:, 512:768] = low
    loads[4].wait()
    high, low = split(cy[...])
    cy3[0:256] = high
    cy3[256:512] = high
    cy3[512:768] = low
    takes[2].wait()
    biases = [jnp.concatenate([bias[l : l + 1], bias[l : l + 1]], axis=1) for l in range(3)]

    def edge_row(e, with_tangent):
        put_taps(xq, e, x[e, 0].astype(F32) * valid(e))
        if with_tangent:
            put_taps(tq, e, x[e, 1].astype(F32) * valid(e))

    def activation(l, z, e, s_buf, i, out):
        h = jnp.tanh(z + biases[l])
        s = 1.0 - h * h
        if not inner(e):
            mask = pair_mask(e)
            s = s * mask
            h = h * mask
        s_buf[i] = s
        if out is not None:
            put_three(out, i, h)
        return s

    def layer_one(i, tangent):
        s = activation(0, thin_conv(xq, 2 * i, w1), 2 * i + 1, s1, i, a1)
        if tangent:
            put_three(t1, i, s * thin_conv(tq, 2 * i, w1))

    def layer_two(i, tangent):
        s = activation(1, wide_conv(a1, i, wk2), 2 * i + 2, s2, i, a2)
        if tangent:
            put_three(t2, i, s * wide_conv(t1, i, wk2))

    def layer_three(i, tangent):
        s = activation(2, wide_conv(a2, i, wk3), 2 * i + 3, s3, i, None)
        if tangent:
            t3[i] = (s * wide_conv(t2, i, wk3)).astype(BF16)

    layer_one(3, True)
    for copy in halo[:2]:
        copy.wait_recv()

    for e in (2, 3, 4, 5, 10, 11, 12, 13):
        edge_row(e, True)
    for i in (1, 2, 4, 5):
        layer_one(i, True)
    for i in range(1, 5):
        layer_two(i, True)
    for i in range(1, 4):
        layer_three(i, True)

    last = wl[...].reshape(144, 128)
    parts = []
    for i in range(1, 4):
        for half in range(2):
            parts.append(contract(last, t3[i, :, half * 128 : half * 128 + 128], ((1,), (1,))))
    for r in range(4):
        chg[:, r, :] = fold_rows(parts, r, False)

    @pl.when(has_next)
    def _():
        ahead.wait_recv()

    @pl.when(tm == WINDOWS - 1)
    def _():
        nxt[...] = jnp.zeros(nxt.shape, F32)

    misfit = nxt[...] - inc[0] - chg[...]
    high, low = split(misfit.reshape(64, 256))
    smoothed = contract(jnp.concatenate([high, low, high], axis=1), cy3[...])
    for half in range(2):
        sbuf[half * 16 : half * 16 + 16] = smoothed[:, half * 128 : half * 128 + 128].reshape(
            16, 4, 128
        )

    hear(1)

    def chip_at(dz, dx):
        return lax.rem(lax.div(chip, 4) + dz, 8) * 4 + lax.rem(chip + dx, 4)

    def out_chunk(c, send, recv):
        return pltpu.make_async_remote_copy(
            sbuf.at[c], rbuf.at[me], send, recv,
            device_id={"tile": 2 * c}, device_id_type=MESH,
        )

    for dz, dx in FAR_FIRST:
        out_chunk(chip_at(dz, dx), as_, ar).start()
    own_chunk = pltpu.make_async_copy(sbuf.at[chip], rbuf.at[me], al)

    @pl.when(core == 0)
    def _():
        own_chunk.start()

    @pl.when(core == 1)
    def _():
        out_chunk(chip, at_s, at_r).start()

    for copy in halo[2:]:
        copy.wait_recv()
    for e in (0, 1, 14, 15):
        edge_row(e, False)
    for i in (0, 6):
        layer_one(i, False)
    for i in (0, 5):
        layer_two(i, False)
    for i in (0, 4):
        layer_three(i, False)
    build_wide(vk3, lambda t: wm[1, 8 - t].T)
    build_wide(vk2, lambda t: wm[0, 8 - t].T)

    @pl.when(core == 0)
    def _():
        obuf[0, 0] = jnp.zeros((4, 128), BF16)
        obuf[TILES - 1, 1] = jnp.zeros((4, 128), BF16)
        own_chunk.wait()
        partner = pltpu.make_async_remote_copy(
            sbuf.at[0], rbuf.at[me + 1], at_s, at_r,
            device_id={"tile": me}, device_id_type=MESH,
        )
        partner.wait_recv()
        pltpu.make_async_copy(
            rbuf.at[0 : TILES - 2], rbuf.at[0 : TILES - 2], ar
        ).wait()
        high, low = split(rbuf[...].reshape(256, 128))
        result = contract(cx3[...], jnp.concatenate([high, low, high], axis=0))
        high, low = split(result)
        high = high.reshape(TILES, 4, 128)
        obuf[1:TILES, 0] = high[0 : TILES - 1]
        obuf[0 : TILES - 1, 1] = high[1:TILES]
        obuf[:, 2] = high
        obuf[:, 3] = low.reshape(TILES, 4, 128)

        def back_chunk(d, send, recv):
            return pltpu.make_async_remote_copy(
                obuf.at[d], mbuf.at[chip], send, recv,
                device_id={"tile": d}, device_id_type=MESH,
            )

        for dz, dx in FAR_FIRST:
            c = chip_at(dz, dx)
            for half in range(2):
                back_chunk(2 * c + half, bs, br).start()
        back_chunk(me + 1, bt_s, bt_r).start()
        own_back = pltpu.make_async_copy(obuf.at[me], mbuf.at[chip], bl)
        own_back.start()
        own_back.wait()

    @pl.when(core == 1)
    def _():
        pltpu.make_async_remote_copy(
            obuf.at[0], mbuf.at[chip], bt_s, bt_r,
            device_id={"tile": me}, device_id_type=MESH,
        ).wait_recv()

    pltpu.make_async_copy(mbuf.at[0 : CHIPS - 1], mbuf.at[0 : CHIPS - 1], br).wait()

    behind = pltpu.make_async_remote_copy(
        mbuf.at[:, 2:4], prev, ps, pr, device_id={"tm": tm_next}, device_id_type=MESH
    )

    @pl.when(has_next)
    def _():
        behind.start()


    for half in range(2):
        lanes = slice(half * 128, half * 128 + 128)
        chunk = slice(half * 16, half * 16 + 16)
        for j, slot in enumerate((0, 2, 1)):
            bx[j, :, :, lanes] = mbuf[chunk, slot].astype(F32)
        high_o[0, :, :, lanes] = mbuf[chunk, 2]
        low_o[0, :, :, lanes] = mbuf[chunk, 3]

    for idx in range(12):
        j, k = idx // 4, idx % 4
        row = bx[j, :, k, :]
        if j != 1:
            row = row * valid(2 + idx)
        put_taps(xq, idx, row)
    for i in range(5):
        b = s3[i] * thin_conv(xq, 2 * i, v4)
        put_three(b3, i, b)
    for i in range(4):
        put_three(b2, i, s2[i + 1] * wide_conv(b3, i, vk3))
    for i in range(3):
        b1[i] = (s1[i + 2] * wide_conv(b2, i, vk2)).astype(BF16)
    first = wf[...].reshape(144, 128)
    parts = []
    for i in range(3):
        for half in range(2):
            parts.append(contract(first, b1[i, :, half * 128 : half * 128 + 128], ((1,), (1,))))
    for r in range(4):
        chg[:, r, :] = fold_rows(parts, r, True)

    @pl.when(has_back)
    def _():
        behind.wait_recv()

    @pl.when(tm == 0)
    def _():
        prev[...] = jnp.zeros(prev.shape, BF16)

    for half in range(2):
        lanes = slice(half * 128, half * 128 + 128)
        chunk = slice(half * 16, half * 16 + 16)
        earlier = prev[chunk, 0].astype(F32) + prev[chunk, 1].astype(F32)
        rest_o[0, :, :, lanes] = earlier - chg[:, :, lanes]

    for copy in halo:
        copy.wait_send()

    @pl.when(has_back)
    def _():
        ahead.wait_send()

    @pl.when(has_next)
    def _():
        behind.wait_send()

    pltpu.make_async_copy(sbuf.at[0 : CHIPS - 1], sbuf.at[0 : CHIPS - 1], as_).wait()

    @pl.when(core == 1)
    def _():
        pltpu.make_async_copy(sbuf.at[0], sbuf.at[0], at_s).wait()

    @pl.when(core == 0)
    def _():
        pltpu.make_async_copy(obuf.at[0], obuf.at[0], bt_s).wait()
        sent = mbuf.at[0 : CHIPS - 1]
        pltpu.make_async_copy(sent, sent, bs).wait()
        pltpu.make_async_copy(sent, sent, bs).wait()


def local(states, increments, w_first, w_mid, w_last, biases, cov_x, cov_y):
    anywhere = pl.BlockSpec(memory_space=pl.ANY)
    dma = pltpu.SemaphoreType.DMA
    scratch = [
        pltpu.VMEM((1, 16, 4, 256), F32),
        pltpu.VMEM((1, 16, 4, 256), F32),
        pltpu.VMEM((3, 128), F32),
        pltpu.VMEM((9, 16, 128), BF16),
        pltpu.VMEM((2, 9, 128, 128), BF16),
        pltpu.VMEM((9, 16, 128), BF16),
        pltpu.VMEM((256, 256), F32),
        pltpu.VMEM((256, 256), F32),
        pltpu.VMEM((16, 2, 16, 256), BF16),
        pltpu.VMEM((16, 48, 256), BF16),
        pltpu.VMEM((16, 48, 256), BF16),
        pltpu.VMEM((7, 256, 768), BF16),
        pltpu.VMEM((7, 256, 768), BF16),
        pltpu.VMEM((6, 256, 768), BF16),
        pltpu.VMEM((6, 256, 768), BF16),
        pltpu.VMEM((5, 256, 256), BF16),
        pltpu.VMEM((5, 256, 768), BF16),
        pltpu.VMEM((4, 256, 768), BF16),
        pltpu.VMEM((3, 256, 256), BF16),
        pltpu.VMEM((7, 256, 256), F32),
        pltpu.VMEM((6, 256, 256), F32),
        pltpu.VMEM((5, 256, 256), F32),
        pltpu.VMEM((192, 256), BF16),
        pltpu.VMEM((1536, 256), BF16),
        pltpu.VMEM((1536, 256), BF16),
        pltpu.VMEM((192, 256), BF16),
        pltpu.VMEM((1536, 256), BF16),
        pltpu.VMEM((1536, 256), BF16),
        pltpu.VMEM((256, 768), BF16),
        pltpu.VMEM((768, 256), BF16),
        pltpu.VMEM((16, 4, 256), F32),
        pltpu.VMEM((32, 2, 4, 128), BF16),
        pltpu.VMEM((16, 4, 256), F32),
        pltpu.VMEM((3, 16, 4, 256), F32),
        pltpu.VMEM((32, 4, 128), F32),
        pltpu.VMEM((TILES, 4, 128), F32),
        pltpu.VMEM((TILES, 4, 4, 128), BF16),
        pltpu.VMEM((32, 4, 4, 128), BF16),
        dma((3,)), dma((5,)), pltpu.SemaphoreType.REGULAR((2,)),
        dma((4,)), dma((4,)),
        dma, dma, dma, dma,
        dma, dma, dma, dma, dma,
        dma, dma, dma, dma, dma,
    ]
    high, low, rest = pl.pallas_call(
        kernel,
        out_shape=[
            pltpu.VMEM(states.shape, BF16),
            pltpu.VMEM(states.shape, BF16),
            pltpu.VMEM(states.shape, F32),
        ],
        in_specs=[anywhere] * 8,
        out_specs=[pl.BlockSpec(memory_space=pltpu.VMEM)] * 3,
        scratch_shapes=scratch,
        compiler_params=pltpu.CompilerParams(collective_id=0, has_side_effects=True),
    )(states, increments, w_first, w_mid, w_last, biases, cov_x, cov_y)
    multiplier = high.astype(F32) + low.astype(F32)
    return multiplier, rest - multiplier


def solution(mesh):
    block = P("tm", None, "tile", None)
    return jax.shard_map(
        local,
        mesh=mesh,
        in_specs=(block, block, P(), P(), P(), P(), P(), P()),
        out_specs=(block, block),
        check_vma=False,
    )
```

```python
import jax
import jax.numpy as jnp
from jax import lax
from jax.experimental import pallas as pl
from jax.experimental.pallas import tpu as pltpu
from jax.sharding import PartitionSpec as P

F32 = jnp.float32
BF16 = jnp.bfloat16
MESH = pl.DeviceIdType.MESH
TILES = 64
WINDOWS = 4
CHIPS = 32
FAR_FIRST = sorted(
    ((z, x) for z in range(8) for x in range(4) if z or x),
    key=lambda s: -(min(s[0], 8 - s[0]) + min(s[1], 4 - s[1])),
)
EARLY_FIRST = (0, 1, 2, 3, 7, 4, 6, 5)


def contract(a, b, dims=((1,), (0,))):
    return lax.dot_general(a, b, (dims, ((), ())), preferred_element_type=F32)


def split(x):
    high = x.astype(BF16)
    return high, (x - high.astype(F32)).astype(BF16)


def shifted_rows(v):
    at = lax.broadcasted_iota(jnp.int32, (8, v.shape[1]), 0)
    up = pltpu.roll(v, 1, 0)
    down = pltpu.roll(v, v.shape[0] - 1, 0)
    up = jnp.concatenate([jnp.where(at == 0, 0.0, up[:8]), up[8:]], axis=0)
    down = jnp.concatenate([down[:-8], jnp.where(at == 7, 0.0, down[-8:])], axis=0)
    return up, down


def shifted_lanes(v):
    at = lax.broadcasted_iota(jnp.int32, v.shape, 1)
    n = v.shape[1]
    up = jnp.where(at == 0, 0.0, pltpu.roll(v, 1, 1))
    down = jnp.where(at == n - 1, 0.0, pltpu.roll(v, n - 1, 1))
    return up, down


def put_three(buf, i, v):
    up, down = shifted_rows(v)
    buf[i, :, 0:256] = up.astype(BF16)
    buf[i, :, 256:512] = v.astype(BF16)
    buf[i, :, 512:768] = down.astype(BF16)


def put_taps(buf, i, v):
    up, down = shifted_lanes(v)
    buf[i, 0:16] = up.astype(BF16)
    buf[i, 16:32] = v.astype(BF16)
    buf[i, 32:48] = down.astype(BF16)


def build_thin(dst, tap):
    zero = jnp.zeros((16, 128), BF16)
    for r in range(4):
        for q in range(3):
            for o in range(2):
                p = r - o
                at = (r * 3 + q) * 16
                block = tap(3 * p + q) if 0 <= p <= 2 else zero
                dst[at : at + 16, o * 128 : o * 128 + 128] = block


def build_wide(dst, tap):
    zero = jnp.zeros((128, 128), BF16)
    for pair in range(2):
        for q in range(3):
            for rr in range(2):
                for o in range(2):
                    p = 2 * pair + rr - o
                    at = pair * 768 + q * 256 + rr * 128
                    block = tap(3 * p + q) if 0 <= p <= 2 else zero
                    dst[at : at + 128, o * 128 : o * 128 + 128] = block


def wide_conv(buf, i, weights):
    both = jnp.concatenate([buf[i], buf[i + 1]], axis=1)
    return contract(both, weights[...])


def thin_conv(buf, i, weights):
    return contract(buf[i : i + 4].reshape(192, 256), weights[...], ((0,), (0,)))


def fold_rows(parts, r, flipped):
    sums = []
    for q in range(3):
        total = None
        for p in range(3):
            t = 3 * p + q
            t = 8 - t if flipped else t
            piece = parts[r + p][t * 16 : t * 16 + 16]
            total = piece if total is None else total + piece
        sums.append(total)
    up, _ = shifted_lanes(sums[0])
    _, down = shifted_lanes(sums[2])
    return up + sums[1] + down


def kernel(
    st_h, inc_h, wf_h, wm_h, wl_h, bias_h, cx_h, cy_h,
    high_o, low_o, rest_o,
    st, inc, bias, wf, wm, wl, cx, cy,
    x, xq, tq, a1, t1, a2, t2, t3, b3, b2, b1, s1, s2, s3,
    w1, wk2, wk3, v4, vk3, vk2, cx3, cy3,
    nxt, prev, chg, bx, sbuf, rbuf, obuf, mbuf,
    insem, wsem, near, hs, hr, ns, nr, ps, pr, as_, ar, at_s, at_r, al, bs, br, bt_s, bt_r, bl,
):
    tm = lax.axis_index("tm")
    me = lax.axis_index("tile")
    chip = lax.div(me, 2)
    core = lax.rem(me, 2)
    has_next = tm < WINDOWS - 1
    has_back = tm > 0
    tm_next = jnp.minimum(tm + 1, WINDOWS - 1)
    tm_back = jnp.maximum(tm - 1, 0)

    def tile_at(step):
        return lax.rem(me + (step + TILES), TILES)

    barrier = pltpu.get_barrier_semaphore()
    def greet(to):
        pl.semaphore_signal(barrier, inc=1, device_id={"tile": to}, device_id_type=MESH)

    for step in (1, -1, 2, -2, 8, -8, 16, -16):
        greet(tile_at(step))
    for step in range(1, 8):
        greet(lax.div(me, 8) * 8 + lax.rem(me + step, 8))

    @pl.when(has_next)
    def _():
        pl.semaphore_signal(
            barrier, inc=1, device_id={"tm": tm_next}, device_id_type=MESH
        )

    takes = [
        pltpu.make_async_copy(src, dst, insem.at[n])
        for n, (src, dst) in enumerate(((st_h, st), (inc_h, inc), (bias_h, bias)))
    ]
    loads = [
        pltpu.make_async_copy(src, dst, wsem.at[n])
        for n, (src, dst) in enumerate(
            ((wf_h, wf), (wm_h, wm), (wl_h, wl), (cx_h, cx), (cy_h, cy))
        )
    ]
    for load in takes + loads:
        load.start()

    def tell(n):
        for step in (8, -8, 16, -16):
            pl.semaphore_signal(
                near.at[n], inc=1, device_id={"tile": tile_at(step)}, device_id_type=MESH
            )

    def hear(n):
        pl.semaphore_wait(near.at[n], 4)

    takes[0].wait()
    for r in range(4):
        x[6 + r, 0] = st[0, :, r, :].astype(BF16)
    takes[1].wait()
    for r in range(4):
        x[6 + r, 1] = inc[0, :, r, :].astype(BF16)

    pl.semaphore_wait(barrier, jnp.where(has_back, 16, 15))

    halo = []
    for n, (step, src, dst) in enumerate(
        (
            (1, x.at[6:10], x.at[2:6]),
            (TILES - 1, x.at[6:10], x.at[10:14]),
            (2, x.at[8:10, 0], x.at[0:2, 0]),
            (TILES - 2, x.at[6:8, 0], x.at[14:16, 0]),
        )
    ):
        halo.append(
            pltpu.make_async_remote_copy(
                src, dst, hs.at[n], hr.at[n],
                device_id={"tile": lax.rem(me + step, TILES)}, device_id_type=MESH,
            )
        )
    for copy in halo:
        copy.start()
    ahead = pltpu.make_async_remote_copy(
        inc.at[0], nxt, ns, nr, device_id={"tm": tm_back}, device_id_type=MESH
    )
    tell(0)

    @pl.when(has_back)
    def _():
        ahead.start()


    def valid(e):
        g = 4 * me - 6 + e
        return jnp.where((g >= 0) & (g < 4 * TILES), 1.0, 0.0).astype(F32)

    def pair_mask(e):
        lane = lax.broadcasted_iota(jnp.int32, (1, 256), 1)
        return jnp.where(lane < 128, valid(e), valid(e + 1))

    def inner(e):
        return e >= 6 and e + 1 <= 9

    for e in range(6, 10):
        put_taps(xq, e, x[e, 0].astype(F32))
        put_taps(tq, e, x[e, 1].astype(F32))
    loads[0].wait()
    build_thin(w1, lambda t: wf[t])
    hear(0)
    tell(1)
    takes[2].wait()
    biases = [jnp.concatenate([bias[l : l + 1], bias[l : l + 1]], axis=1) for l in range(3)]

    def edge_row(e, with_tangent):
        put_taps(xq, e, x[e, 0].astype(F32) * valid(e))
        if with_tangent:
            put_taps(tq, e, x[e, 1].astype(F32) * valid(e))

    def activation(l, z, e, s_buf, i, out):
        h = jnp.tanh(z + biases[l])
        s = 1.0 - h * h
        if not inner(e):
            mask = pair_mask(e)
            s = s * mask
            h = h * mask
        s_buf[i] = s
        if out is not None:
            put_three(out, i, h)
        return s

    def layer_one(i, tangent):
        s = activation(0, thin_conv(xq, 2 * i, w1), 2 * i + 1, s1, i, a1)
        if tangent:
            put_three(t1, i, s * thin_conv(tq, 2 * i, w1))

    def layer_two(i, tangent):
        s = activation(1, wide_conv(a1, i, wk2), 2 * i + 2, s2, i, a2)
        if tangent:
            put_three(t2, i, s * wide_conv(t1, i, wk2))

    def layer_three(i, tangent):
        s = activation(2, wide_conv(a2, i, wk3), 2 * i + 3, s3, i, None)
        if tangent:
            t3[i] = (s * wide_conv(t2, i, wk3)).astype(BF16)

    layer_one(3, True)
    loads[1].wait()
    build_wide(wk2, lambda t: wm[0, t])

    def side(upper):
        halo[1 if upper else 0].wait_recv()
        for e in (10, 11, 12, 13) if upper else (5, 4, 3, 2):
            edge_row(e, True)
        for i in (4, 5) if upper else (2, 1):
            layer_one(i, True)

    def near_side(upper):
        side(upper)
        for i in (3, 4) if upper else (2, 1):
            layer_two(i, True)
        build_wide(wk3, lambda t: wm[1, t])
        layer_three(3 if upper else 1, True)

    def far_side(upper):
        side(upper)
        for i in (3, 4) if upper else (2, 1):
            layer_two(i, True)
        for i in (2, 3) if upper else (2, 1):
            layer_three(i, True)

    @pl.when(core == 0)
    def _():
        near_side(True)

    @pl.when(core == 1)
    def _():
        near_side(False)

    loads[2].wait()
    loads[4].wait()
    high, low = split(cy[...])
    cy3[0:256] = high
    cy3[256:512] = high
    cy3[512:768] = low

    @pl.when(core == 0)
    def _():
        far_side(False)

    @pl.when(core == 1)
    def _():
        far_side(True)

    last = wl[...].reshape(144, 128)
    parts = []
    for i in range(1, 4):
        for half in range(2):
            parts.append(contract(last, t3[i, :, half * 128 : half * 128 + 128], ((1,), (1,))))
    for r in range(4):
        chg[:, r, :] = fold_rows(parts, r, False)

    @pl.when(has_next)
    def _():
        ahead.wait_recv()

    @pl.when(tm == WINDOWS - 1)
    def _():
        nxt[...] = jnp.zeros(nxt.shape, F32)

    misfit = nxt[...] - inc[0] - chg[...]
    high, low = split(misfit.reshape(64, 256))
    smoothed = contract(jnp.concatenate([high, low, high], axis=1), cy3[...])
    for half in range(2):
        sbuf[half * 16 : half * 16 + 16] = smoothed[:, half * 128 : half * 128 + 128].reshape(
            16, 4, 128
        )

    hear(1)

    def chip_at(dz, dx):
        return lax.rem(lax.div(chip, 4) + dz, 8) * 4 + lax.rem(chip + dx, 4)

    def out_chunk(c, send, recv):
        return pltpu.make_async_remote_copy(
            sbuf.at[c], rbuf.at[me], send, recv,
            device_id={"tile": 2 * c}, device_id_type=MESH,
        )

    for dz, dx in FAR_FIRST:
        out_chunk(chip_at(dz, dx), as_, ar).start()
    own_chunk = pltpu.make_async_copy(sbuf.at[chip], rbuf.at[me], al)

    @pl.when(core == 0)
    def _():
        own_chunk.start()

    @pl.when(core == 1)
    def _():
        out_chunk(chip, at_s, at_r).start()

    loads[3].wait()
    high, low = split(cx[...])
    cx3[:, 0:256] = high
    cx3[:, 256:512] = high
    cx3[:, 512:768] = low

    for copy in halo[2:]:
        copy.wait_recv()
    for e in (0, 1, 14, 15):
        edge_row(e, False)
    for i in (0, 6):
        layer_one(i, False)
    for i in (0, 5):
        layer_two(i, False)
    for i in (0, 4):
        layer_three(i, False)
    build_thin(v4, lambda t: wl[8 - t])
    build_wide(vk3, lambda t: wm[1, 8 - t].T)
    build_wide(vk2, lambda t: wm[0, 8 - t].T)

    @pl.when(core == 0)
    def _():
        obuf[0, 0] = jnp.zeros((4, 128), BF16)
        obuf[TILES - 1, 1] = jnp.zeros((4, 128), BF16)
        own_chunk.wait()
        partner = pltpu.make_async_remote_copy(
            sbuf.at[0], rbuf.at[me + 1], at_s, at_r,
            device_id={"tile": me}, device_id_type=MESH,
        )
        partner.wait_recv()
        pltpu.make_async_copy(
            rbuf.at[0 : TILES - 2], rbuf.at[0 : TILES - 2], ar
        ).wait()
        high, low = split(rbuf[...].reshape(256, 128))
        result = contract(cx3[...], jnp.concatenate([high, low, high], axis=0))
        high, low = split(result)
        high = high.reshape(TILES, 4, 128)
        obuf[1:TILES, 0] = high[0 : TILES - 1]
        obuf[0 : TILES - 1, 1] = high[1:TILES]
        obuf[:, 2] = high
        obuf[:, 3] = low.reshape(TILES, 4, 128)

        def back_chunk(d, send, recv):
            return pltpu.make_async_remote_copy(
                obuf.at[d], mbuf.at[chip], send, recv,
                device_id={"tile": d}, device_id_type=MESH,
            )

        for z in EARLY_FIRST:
            for dx in range(4):
                c = z * 4 + lax.rem(chip + dx, 4)

                @pl.when(c != chip)
                def _():
                    for half in range(2):
                        back_chunk(2 * c + half, bs, br).start()

        back_chunk(me + 1, bt_s, bt_r).start()
        own_back = pltpu.make_async_copy(obuf.at[me], mbuf.at[chip], bl)
        own_back.start()
        own_back.wait()

    @pl.when(core == 1)
    def _():
        pltpu.make_async_remote_copy(
            obuf.at[0], mbuf.at[chip], bt_s, bt_r,
            device_id={"tile": me}, device_id_type=MESH,
        ).wait_recv()

    pltpu.make_async_copy(mbuf.at[0 : CHIPS - 1], mbuf.at[0 : CHIPS - 1], br).wait()

    behind = pltpu.make_async_remote_copy(
        mbuf.at[:, 2:4], prev, ps, pr, device_id={"tm": tm_next}, device_id_type=MESH
    )

    @pl.when(has_next)
    def _():
        behind.start()


    for half in range(2):
        lanes = slice(half * 128, half * 128 + 128)
        chunk = slice(half * 16, half * 16 + 16)
        for j, slot in enumerate((0, 2, 1)):
            bx[j, :, :, lanes] = mbuf[chunk, slot].astype(F32)
        high_o[0, :, :, lanes] = mbuf[chunk, 2]
        low_o[0, :, :, lanes] = mbuf[chunk, 3]

    for idx in range(12):
        j, k = idx // 4, idx % 4
        row = bx[j, :, k, :]
        if j != 1:
            row = row * valid(2 + idx)
        put_taps(xq, idx, row)
    for i in range(5):
        b = s3[i] * thin_conv(xq, 2 * i, v4)
        put_three(b3, i, b)
    for i in range(4):
        put_three(b2, i, s2[i + 1] * wide_conv(b3, i, vk3))
    for i in range(3):
        b1[i] = (s1[i + 2] * wide_conv(b2, i, vk2)).astype(BF16)
    first = wf[...].reshape(144, 128)
    parts = []
    for i in range(3):
        for half in range(2):
            parts.append(contract(first, b1[i, :, half * 128 : half * 128 + 128], ((1,), (1,))))
    for r in range(4):
        chg[:, r, :] = fold_rows(parts, r, True)

    @pl.when(has_back)
    def _():
        behind.wait_recv()

    @pl.when(tm == 0)
    def _():
        prev[...] = jnp.zeros(prev.shape, BF16)

    for half in range(2):
        lanes = slice(half * 128, half * 128 + 128)
        chunk = slice(half * 16, half * 16 + 16)
        earlier = prev[chunk, 0].astype(F32) + prev[chunk, 1].astype(F32)
        rest_o[0, :, :, lanes] = earlier - chg[:, :, lanes]

    for copy in halo:
        copy.wait_send()

    @pl.when(has_back)
    def _():
        ahead.wait_send()

    @pl.when(has_next)
    def _():
        behind.wait_send()

    pltpu.make_async_copy(sbuf.at[0 : CHIPS - 1], sbuf.at[0 : CHIPS - 1], as_).wait()

    @pl.when(core == 1)
    def _():
        pltpu.make_async_copy(sbuf.at[0], sbuf.at[0], at_s).wait()

    @pl.when(core == 0)
    def _():
        pltpu.make_async_copy(obuf.at[0], obuf.at[0], bt_s).wait()
        sent = mbuf.at[0 : CHIPS - 1]
        pltpu.make_async_copy(sent, sent, bs).wait()
        pltpu.make_async_copy(sent, sent, bs).wait()


def local(states, increments, w_first, w_mid, w_last, biases, cov_x, cov_y):
    anywhere = pl.BlockSpec(memory_space=pl.ANY)
    dma = pltpu.SemaphoreType.DMA
    scratch = [
        pltpu.VMEM((1, 16, 4, 256), F32),
        pltpu.VMEM((1, 16, 4, 256), F32),
        pltpu.VMEM((3, 128), F32),
        pltpu.VMEM((9, 16, 128), BF16),
        pltpu.VMEM((2, 9, 128, 128), BF16),
        pltpu.VMEM((9, 16, 128), BF16),
        pltpu.VMEM((256, 256), F32),
        pltpu.VMEM((256, 256), F32),
        pltpu.VMEM((16, 2, 16, 256), BF16),
        pltpu.VMEM((16, 48, 256), BF16),
        pltpu.VMEM((16, 48, 256), BF16),
        pltpu.VMEM((7, 256, 768), BF16),
        pltpu.VMEM((7, 256, 768), BF16),
        pltpu.VMEM((6, 256, 768), BF16),
        pltpu.VMEM((6, 256, 768), BF16),
        pltpu.VMEM((5, 256, 256), BF16),
        pltpu.VMEM((5, 256, 768), BF16),
        pltpu.VMEM((4, 256, 768), BF16),
        pltpu.VMEM((3, 256, 256), BF16),
        pltpu.VMEM((7, 256, 256), F32),
        pltpu.VMEM((6, 256, 256), F32),
        pltpu.VMEM((5, 256, 256), F32),
        pltpu.VMEM((192, 256), BF16),
        pltpu.VMEM((1536, 256), BF16),
        pltpu.VMEM((1536, 256), BF16),
        pltpu.VMEM((192, 256), BF16),
        pltpu.VMEM((1536, 256), BF16),
        pltpu.VMEM((1536, 256), BF16),
        pltpu.VMEM((256, 768), BF16),
        pltpu.VMEM((768, 256), BF16),
        pltpu.VMEM((16, 4, 256), F32),
        pltpu.VMEM((32, 2, 4, 128), BF16),
        pltpu.VMEM((16, 4, 256), F32),
        pltpu.VMEM((3, 16, 4, 256), F32),
        pltpu.VMEM((32, 4, 128), F32),
        pltpu.VMEM((TILES, 4, 128), F32),
        pltpu.VMEM((TILES, 4, 4, 128), BF16),
        pltpu.VMEM((32, 4, 4, 128), BF16),
        dma((3,)), dma((5,)), pltpu.SemaphoreType.REGULAR((2,)),
        dma((4,)), dma((4,)),
        dma, dma, dma, dma,
        dma, dma, dma, dma, dma,
        dma, dma, dma, dma, dma,
    ]
    high, low, rest = pl.pallas_call(
        kernel,
        out_shape=[
            pltpu.VMEM(states.shape, BF16),
            pltpu.VMEM(states.shape, BF16),
            pltpu.VMEM(states.shape, F32),
        ],
        in_specs=[anywhere] * 8,
        out_specs=[pl.BlockSpec(memory_space=pltpu.VMEM)] * 3,
        scratch_shapes=scratch,
        compiler_params=pltpu.CompilerParams(collective_id=0, has_side_effects=True),
    )(states, increments, w_first, w_mid, w_last, biases, cov_x, cov_y)
    multiplier = high.astype(F32) + low.astype(F32)
    return multiplier, rest - multiplier


def solution(mesh):
    block = P("tm", None, "tile", None)
    return jax.shard_map(
        local,
        mesh=mesh,
        in_specs=(block, block, P(), P(), P(), P(), P(), P()),
        out_specs=(block, block),
        check_vma=False,
    )
```

```python
import jax
import jax.numpy as jnp
from jax import lax
from jax.experimental import pallas as pl
from jax.experimental.pallas import tpu as pltpu
from jax.sharding import PartitionSpec as P

F32 = jnp.float32
BF16 = jnp.bfloat16
MESH = pl.DeviceIdType.MESH
TILES = 64
WINDOWS = 4
CHIPS = 32
FAR_FIRST = sorted(
    ((z, x) for z in range(8) for x in range(4) if z or x),
    key=lambda s: -(min(s[0], 8 - s[0]) + min(s[1], 4 - s[1])),
)
EARLY_FIRST = (0, 1, 2, 3, 7, 4, 6, 5)


def contract(a, b, dims=((1,), (0,))):
    return lax.dot_general(a, b, (dims, ((), ())), preferred_element_type=F32)


def split(x):
    high = x.astype(BF16)
    return high, (x - high.astype(F32)).astype(BF16)


def shifted_rows(v):
    at = lax.broadcasted_iota(jnp.int32, (8, v.shape[1]), 0)
    up = pltpu.roll(v, 1, 0)
    down = pltpu.roll(v, v.shape[0] - 1, 0)
    up = jnp.concatenate([jnp.where(at == 0, 0.0, up[:8]), up[8:]], axis=0)
    down = jnp.concatenate([down[:-8], jnp.where(at == 7, 0.0, down[-8:])], axis=0)
    return up, down


def shifted_lanes(v):
    at = lax.broadcasted_iota(jnp.int32, v.shape, 1)
    n = v.shape[1]
    up = jnp.where(at == 0, 0.0, pltpu.roll(v, 1, 1))
    down = jnp.where(at == n - 1, 0.0, pltpu.roll(v, n - 1, 1))
    return up, down


def put_three(buf, i, v):
    up, down = shifted_rows(v)
    buf[i, :, 0:256] = up.astype(BF16)
    buf[i, :, 256:512] = v.astype(BF16)
    buf[i, :, 512:768] = down.astype(BF16)


def put_taps(buf, i, v):
    up, down = shifted_lanes(v)
    buf[i, 0:16] = up.astype(BF16)
    buf[i, 16:32] = v.astype(BF16)
    buf[i, 32:48] = down.astype(BF16)


def build_thin(dst, tap):
    zero = jnp.zeros((16, 128), BF16)
    for r in range(4):
        for q in range(3):
            for o in range(2):
                p = r - o
                at = (r * 3 + q) * 16
                block = tap(3 * p + q) if 0 <= p <= 2 else zero
                dst[at : at + 16, o * 128 : o * 128 + 128] = block


def build_wide(dst, tap):
    zero = jnp.zeros((128, 128), BF16)
    for pair in range(2):
        for q in range(3):
            for rr in range(2):
                for o in range(2):
                    p = 2 * pair + rr - o
                    at = pair * 768 + q * 256 + rr * 128
                    block = tap(3 * p + q) if 0 <= p <= 2 else zero
                    dst[at : at + 128, o * 128 : o * 128 + 128] = block


def wide_conv(buf, i, weights):
    both = jnp.concatenate([buf[i], buf[i + 1]], axis=1)
    return contract(both, weights[...])


def thin_conv(buf, i, weights):
    return contract(buf[i : i + 4].reshape(192, 256), weights[...], ((0,), (0,)))


def fold_rows(parts, r, flipped):
    sums = []
    for q in range(3):
        total = None
        for p in range(3):
            t = 3 * p + q
            t = 8 - t if flipped else t
            piece = parts[r + p][t * 16 : t * 16 + 16]
            total = piece if total is None else total + piece
        sums.append(total)
    up, _ = shifted_lanes(sums[0])
    _, down = shifted_lanes(sums[2])
    return up + sums[1] + down


def kernel(
    st_h, inc_h, wf_h, wm_h, wl_h, bias_h, cx_h, cy_h,
    high_o, low_o, rest_o,
    st, inc, bias, wf, wm, wl, cx, cy,
    x, xq, tq, a1, t1, a2, t2, t3, b3, b2, b1, s1, s2, s3,
    w1, wk2, wk3, v4, vk3, vk2, cx3, cy3,
    nxt, prev, chg, bx, sbuf, rbuf, obuf, mbuf,
    insem, wsem, near, hs, hr, ns, nr, ps, pr, as_, ar, at_s, at_r, al, bs, br, bt_s, bt_r, bl,
):
    tm = lax.axis_index("tm")
    me = lax.axis_index("tile")
    chip = lax.div(me, 2)
    core = lax.rem(me, 2)
    has_next = tm < WINDOWS - 1
    has_back = tm > 0
    tm_next = jnp.minimum(tm + 1, WINDOWS - 1)
    tm_back = jnp.maximum(tm - 1, 0)

    def tile_at(step):
        return lax.rem(me + (step + TILES), TILES)

    barrier = pltpu.get_barrier_semaphore()
    def greet(to):
        pl.semaphore_signal(barrier, inc=1, device_id={"tile": to}, device_id_type=MESH)

    for step in (1, -1, 2, -2, 8, -8, 16, -16):
        greet(tile_at(step))
    for step in range(1, 8):
        greet(lax.div(me, 8) * 8 + lax.rem(me + step, 8))

    @pl.when(has_next)
    def _():
        pl.semaphore_signal(
            barrier, inc=1, device_id={"tm": tm_next}, device_id_type=MESH
        )

    takes = [
        pltpu.make_async_copy(src, dst, insem.at[n])
        for n, (src, dst) in enumerate(((st_h, st), (inc_h, inc), (bias_h, bias)))
    ]
    loads = [
        pltpu.make_async_copy(src, dst, wsem.at[n])
        for n, (src, dst) in enumerate(
            ((wf_h, wf), (wm_h, wm), (wl_h, wl), (cx_h, cx), (cy_h, cy))
        )
    ]
    for load in takes + loads:
        load.start()

    def tell(n):
        for step in (8, -8, 16, -16):
            pl.semaphore_signal(
                near.at[n], inc=1, device_id={"tile": tile_at(step)}, device_id_type=MESH
            )

    def hear(n):
        pl.semaphore_wait(near.at[n], 4)

    takes[0].wait()
    for r in range(4):
        x[6 + r, 0] = st[0, :, r, :].astype(BF16)
    takes[1].wait()
    for r in range(4):
        x[6 + r, 1] = inc[0, :, r, :].astype(BF16)

    pl.semaphore_wait(barrier, jnp.where(has_back, 16, 15))

    halo = []
    for n, (step, src, dst) in enumerate(
        (
            (1, x.at[6:10], x.at[2:6]),
            (TILES - 1, x.at[6:10], x.at[10:14]),
            (2, x.at[8:10, 0], x.at[0:2, 0]),
            (TILES - 2, x.at[6:8, 0], x.at[14:16, 0]),
        )
    ):
        halo.append(
            pltpu.make_async_remote_copy(
                src, dst, hs.at[n], hr.at[n],
                device_id={"tile": lax.rem(me + step, TILES)}, device_id_type=MESH,
            )
        )
    for copy in halo[:2]:
        copy.start()
    ahead = pltpu.make_async_remote_copy(
        inc.at[0], nxt, ns, nr, device_id={"tm": tm_back}, device_id_type=MESH
    )
    tell(0)

    @pl.when(has_back)
    def _():
        ahead.start()


    def valid(e):
        g = 4 * me - 6 + e
        return jnp.where((g >= 0) & (g < 4 * TILES), 1.0, 0.0).astype(F32)

    def pair_mask(e):
        lane = lax.broadcasted_iota(jnp.int32, (1, 256), 1)
        return jnp.where(lane < 128, valid(e), valid(e + 1))

    def inner(e):
        return e >= 6 and e + 1 <= 9

    for e in range(6, 10):
        put_taps(xq, e, x[e, 0].astype(F32))
        put_taps(tq, e, x[e, 1].astype(F32))
    loads[0].wait()
    build_thin(w1, lambda t: wf[t])
    hear(0)
    tell(1)
    takes[2].wait()
    biases = [jnp.concatenate([bias[l : l + 1], bias[l : l + 1]], axis=1) for l in range(3)]

    def edge_row(e, with_tangent):
        put_taps(xq, e, x[e, 0].astype(F32) * valid(e))
        if with_tangent:
            put_taps(tq, e, x[e, 1].astype(F32) * valid(e))

    def activation(l, z, e, s_buf, i, out):
        h = jnp.tanh(z + biases[l])
        s = 1.0 - h * h
        if not inner(e):
            mask = pair_mask(e)
            s = s * mask
            h = h * mask
        s_buf[i] = s
        if out is not None:
            put_three(out, i, h)
        return s

    def layer_one(i, tangent):
        s = activation(0, thin_conv(xq, 2 * i, w1), 2 * i + 1, s1, i, a1)
        if tangent:
            put_three(t1, i, s * thin_conv(tq, 2 * i, w1))

    def layer_two(i, tangent):
        s = activation(1, wide_conv(a1, i, wk2), 2 * i + 2, s2, i, a2)
        if tangent:
            put_three(t2, i, s * wide_conv(t1, i, wk2))

    def layer_three(i, tangent):
        s = activation(2, wide_conv(a2, i, wk3), 2 * i + 3, s3, i, None)
        if tangent:
            t3[i] = (s * wide_conv(t2, i, wk3)).astype(BF16)

    layer_one(3, True)
    loads[1].wait()
    build_wide(wk2, lambda t: wm[0, t])

    def side(upper):
        halo[1 if upper else 0].wait_recv()
        for e in (10, 11, 12, 13) if upper else (5, 4, 3, 2):
            edge_row(e, True)
        for i in (4, 5) if upper else (2, 1):
            layer_one(i, True)

    def near_side(upper):
        side(upper)
        for i in (3, 4) if upper else (2, 1):
            layer_two(i, True)
        build_wide(wk3, lambda t: wm[1, t])
        layer_three(3 if upper else 1, True)

    def far_side(upper):
        side(upper)
        for i in (3, 4) if upper else (2, 1):
            layer_two(i, True)
        for i in (2, 3) if upper else (2, 1):
            layer_three(i, True)

    @pl.when(core == 0)
    def _():
        near_side(True)

    @pl.when(core == 1)
    def _():
        near_side(False)

    for copy in halo[2:]:
        copy.start()
    loads[2].wait()
    loads[4].wait()
    high, low = split(cy[...])
    cy3[0:256] = high
    cy3[256:512] = high
    cy3[512:768] = low

    @pl.when(core == 0)
    def _():
        far_side(False)

    @pl.when(core == 1)
    def _():
        far_side(True)

    last = wl[...].reshape(144, 128)
    parts = []
    for i in range(1, 4):
        for half in range(2):
            parts.append(contract(last, t3[i, :, half * 128 : half * 128 + 128], ((1,), (1,))))
    for r in range(4):
        chg[:, r, :] = fold_rows(parts, r, False)

    @pl.when(has_next)
    def _():
        ahead.wait_recv()

    @pl.when(tm == WINDOWS - 1)
    def _():
        nxt[...] = jnp.zeros(nxt.shape, F32)

    misfit = nxt[...] - inc[0] - chg[...]
    high, low = split(misfit.reshape(64, 256))
    smoothed = contract(jnp.concatenate([high, low, high], axis=1), cy3[...])
    for half in range(2):
        sbuf[half * 16 : half * 16 + 16] = smoothed[:, half * 128 : half * 128 + 128].reshape(
            16, 4, 128
        )

    hear(1)

    def chip_at(dz, dx):
        return lax.rem(lax.div(chip, 4) + dz, 8) * 4 + lax.rem(chip + dx, 4)

    def out_chunk(c, send, recv):
        return pltpu.make_async_remote_copy(
            sbuf.at[c], rbuf.at[me], send, recv,
            device_id={"tile": 2 * c}, device_id_type=MESH,
        )

    for dz, dx in FAR_FIRST:
        out_chunk(chip_at(dz, dx), as_, ar).start()
    own_chunk = pltpu.make_async_copy(sbuf.at[chip], rbuf.at[me], al)

    @pl.when(core == 0)
    def _():
        own_chunk.start()

    @pl.when(core == 1)
    def _():
        out_chunk(chip, at_s, at_r).start()

    loads[3].wait()
    high, low = split(cx[...])
    cx3[:, 0:256] = high
    cx3[:, 256:512] = high
    cx3[:, 512:768] = low

    for copy in halo[2:]:
        copy.wait_recv()
    for e in (0, 1, 14, 15):
        edge_row(e, False)
    for i in (0, 6):
        layer_one(i, False)
    for i in (0, 5):
        layer_two(i, False)
    for i in (0, 4):
        layer_three(i, False)
    build_thin(v4, lambda t: wl[8 - t])
    build_wide(vk3, lambda t: wm[1, 8 - t].T)
    build_wide(vk2, lambda t: wm[0, 8 - t].T)

    @pl.when(core == 0)
    def _():
        obuf[0, 0] = jnp.zeros((4, 128), BF16)
        obuf[TILES - 1, 1] = jnp.zeros((4, 128), BF16)
        own_chunk.wait()
        partner = pltpu.make_async_remote_copy(
            sbuf.at[0], rbuf.at[me + 1], at_s, at_r,
            device_id={"tile": me}, device_id_type=MESH,
        )
        partner.wait_recv()
        pltpu.make_async_copy(
            rbuf.at[0 : TILES - 2], rbuf.at[0 : TILES - 2], ar
        ).wait()
        high, low = split(rbuf[...].reshape(256, 128))
        result = contract(cx3[...], jnp.concatenate([high, low, high], axis=0))
        high, low = split(result)
        high = high.reshape(TILES, 4, 128)
        obuf[1:TILES, 0] = high[0 : TILES - 1]
        obuf[0 : TILES - 1, 1] = high[1:TILES]
        obuf[:, 2] = high
        obuf[:, 3] = low.reshape(TILES, 4, 128)

        def back_chunk(d, send, recv):
            return pltpu.make_async_remote_copy(
                obuf.at[d], mbuf.at[chip], send, recv,
                device_id={"tile": d}, device_id_type=MESH,
            )

        for z in EARLY_FIRST:
            for dx in range(4):
                c = z * 4 + lax.rem(chip + dx, 4)

                @pl.when(c != chip)
                def _():
                    for half in range(2):
                        back_chunk(2 * c + half, bs, br).start()

        back_chunk(me + 1, bt_s, bt_r).start()
        own_back = pltpu.make_async_copy(obuf.at[me], mbuf.at[chip], bl)
        own_back.start()
        own_back.wait()

    @pl.when(core == 1)
    def _():
        pltpu.make_async_remote_copy(
            obuf.at[0], mbuf.at[chip], bt_s, bt_r,
            device_id={"tile": me}, device_id_type=MESH,
        ).wait_recv()

    pltpu.make_async_copy(mbuf.at[0 : CHIPS - 1], mbuf.at[0 : CHIPS - 1], br).wait()

    behind = pltpu.make_async_remote_copy(
        mbuf.at[:, 2:4], prev, ps, pr, device_id={"tm": tm_next}, device_id_type=MESH
    )

    @pl.when(has_next)
    def _():
        behind.start()


    for half in range(2):
        lanes = slice(half * 128, half * 128 + 128)
        chunk = slice(half * 16, half * 16 + 16)
        for j, slot in enumerate((0, 2, 1)):
            bx[j, :, :, lanes] = mbuf[chunk, slot].astype(F32)
        high_o[0, :, :, lanes] = mbuf[chunk, 2]
        low_o[0, :, :, lanes] = mbuf[chunk, 3]

    for idx in range(12):
        j, k = idx // 4, idx % 4
        row = bx[j, :, k, :]
        if j != 1:
            row = row * valid(2 + idx)
        put_taps(xq, idx, row)
    for i in range(5):
        b = s3[i] * thin_conv(xq, 2 * i, v4)
        put_three(b3, i, b)
    for i in range(4):
        put_three(b2, i, s2[i + 1] * wide_conv(b3, i, vk3))
    for i in range(3):
        b1[i] = (s1[i + 2] * wide_conv(b2, i, vk2)).astype(BF16)
    first = wf[...].reshape(144, 128)
    parts = []
    for i in range(3):
        for half in range(2):
            parts.append(contract(first, b1[i, :, half * 128 : half * 128 + 128], ((1,), (1,))))
    for r in range(4):
        chg[:, r, :] = fold_rows(parts, r, True)

    @pl.when(has_back)
    def _():
        behind.wait_recv()

    @pl.when(tm == 0)
    def _():
        prev[...] = jnp.zeros(prev.shape, BF16)

    for half in range(2):
        lanes = slice(half * 128, half * 128 + 128)
        chunk = slice(half * 16, half * 16 + 16)
        earlier = prev[chunk, 0].astype(F32) + prev[chunk, 1].astype(F32)
        rest_o[0, :, :, lanes] = earlier - chg[:, :, lanes]

    for copy in halo:
        copy.wait_send()

    @pl.when(has_back)
    def _():
        ahead.wait_send()

    @pl.when(has_next)
    def _():
        behind.wait_send()

    pltpu.make_async_copy(sbuf.at[0 : CHIPS - 1], sbuf.at[0 : CHIPS - 1], as_).wait()

    @pl.when(core == 1)
    def _():
        pltpu.make_async_copy(sbuf.at[0], sbuf.at[0], at_s).wait()

    @pl.when(core == 0)
    def _():
        pltpu.make_async_copy(obuf.at[0], obuf.at[0], bt_s).wait()
        sent = mbuf.at[0 : CHIPS - 1]
        pltpu.make_async_copy(sent, sent, bs).wait()
        pltpu.make_async_copy(sent, sent, bs).wait()


def local(states, increments, w_first, w_mid, w_last, biases, cov_x, cov_y):
    anywhere = pl.BlockSpec(memory_space=pl.ANY)
    dma = pltpu.SemaphoreType.DMA
    scratch = [
        pltpu.VMEM((1, 16, 4, 256), F32),
        pltpu.VMEM((1, 16, 4, 256), F32),
        pltpu.VMEM((3, 128), F32),
        pltpu.VMEM((9, 16, 128), BF16),
        pltpu.VMEM((2, 9, 128, 128), BF16),
        pltpu.VMEM((9, 16, 128), BF16),
        pltpu.VMEM((256, 256), F32),
        pltpu.VMEM((256, 256), F32),
        pltpu.VMEM((16, 2, 16, 256), BF16),
        pltpu.VMEM((16, 48, 256), BF16),
        pltpu.VMEM((16, 48, 256), BF16),
        pltpu.VMEM((7, 256, 768), BF16),
        pltpu.VMEM((7, 256, 768), BF16),
        pltpu.VMEM((6, 256, 768), BF16),
        pltpu.VMEM((6, 256, 768), BF16),
        pltpu.VMEM((5, 256, 256), BF16),
        pltpu.VMEM((5, 256, 768), BF16),
        pltpu.VMEM((4, 256, 768), BF16),
        pltpu.VMEM((3, 256, 256), BF16),
        pltpu.VMEM((7, 256, 256), F32),
        pltpu.VMEM((6, 256, 256), F32),
        pltpu.VMEM((5, 256, 256), F32),
        pltpu.VMEM((192, 256), BF16),
        pltpu.VMEM((1536, 256), BF16),
        pltpu.VMEM((1536, 256), BF16),
        pltpu.VMEM((192, 256), BF16),
        pltpu.VMEM((1536, 256), BF16),
        pltpu.VMEM((1536, 256), BF16),
        pltpu.VMEM((256, 768), BF16),
        pltpu.VMEM((768, 256), BF16),
        pltpu.VMEM((16, 4, 256), F32),
        pltpu.VMEM((32, 2, 4, 128), BF16),
        pltpu.VMEM((16, 4, 256), F32),
        pltpu.VMEM((3, 16, 4, 256), F32),
        pltpu.VMEM((32, 4, 128), F32),
        pltpu.VMEM((TILES, 4, 128), F32),
        pltpu.VMEM((TILES, 4, 4, 128), BF16),
        pltpu.VMEM((32, 4, 4, 128), BF16),
        dma((3,)), dma((5,)), pltpu.SemaphoreType.REGULAR((2,)),
        dma((4,)), dma((4,)),
        dma, dma, dma, dma,
        dma, dma, dma, dma, dma,
        dma, dma, dma, dma, dma,
    ]
    high, low, rest = pl.pallas_call(
        kernel,
        out_shape=[
            pltpu.VMEM(states.shape, BF16),
            pltpu.VMEM(states.shape, BF16),
            pltpu.VMEM(states.shape, F32),
        ],
        in_specs=[anywhere] * 8,
        out_specs=[pl.BlockSpec(memory_space=pltpu.VMEM)] * 3,
        scratch_shapes=scratch,
        compiler_params=pltpu.CompilerParams(collective_id=0, has_side_effects=True),
    )(states, increments, w_first, w_mid, w_last, biases, cov_x, cov_y)
    multiplier = high.astype(F32) + low.astype(F32)
    return multiplier, rest - multiplier


def solution(mesh):
    block = P("tm", None, "tile", None)
    return jax.shard_map(
        local,
        mesh=mesh,
        in_specs=(block, block, P(), P(), P(), P(), P(), P()),
        out_specs=(block, block),
        check_vma=False,
    )
```
